128 devices in a mesh: row: 8 (over z, core), col: 16 (over x, y).
Axes of the slice: x: 4, y: 4, z: 4, core: 2. Of those that a mesh axis runs over, the one named last changes fastest.
Arguments:
- block_values: bfloat16 [8, 16, 256, 128, 128], P('row', 'col'), may hold values from -1.2 to 1.2
- block_rows: int32 [8, 16, 256], P('row', 'col'), may hold values from 0 to 207, as said below
- block_cols: int32 [8, 16, 256], P('row', 'col'), may hold values from 0 to 103, as said below
- start_vectors: bfloat16 [212992, 256], P(('row', 'col')), may hold values from -6 to 6
- center: float32 [1], replicated, may hold values from -0.5 to -0.1
- half_width: float32 [1], replicated, may hold values from 0.9 to 1.3
- row_counts: int32 [128], replicated, may hold values from 7 to 19, as said below
Outputs:
- relaid: bfloat16 [311296, 256], P(('row', 'col'))
The draws below stay inside these ranges and needn't reach their ends.
Inputs may be any that keep to these rules, and one draw needn't show every extreme that they name: `block_rows`: the first 13 entries of cell (r, c) are its diagonal blocks, at local row c * 13 + k; the rest are anywhere; positions may repeat, and repeated blocks add. `block_cols`: the first 13 entries of cell (r, c) are at local column r * 13 + k. `row_counts`: entries 2 i and 2 i + 1 sum to 26; entry 0 is larger than 13.
All inputs are finite; a program needn't handle non-finite values.
Results may differ from the reference program's by a relative error of at most 0.019.
Values may be sent and summed in bfloat16 or wider, within the bound.
A program may use at most 192 MiB of HBM per device.

```python
import math
import jax
import jax.numpy as jnp
from jax import lax

ORB = 128
VECS = 256
BD = 13
NBD = 256
CAP = 19
ORDER = 212992
N_ROW = 8
N_COL = 16


def block_pattern(key):
    seeded = jax.random.fold_in(key, 7)
    first_key, second_key = jax.random.split(seeded)
    shape = (N_ROW, N_COL, NBD - BD)
    random_rows = jax.random.randint(first_key, shape, 0, N_COL * BD)
    random_cols = jax.random.randint(second_key, shape, 0, N_ROW * BD)
    diagonal = jnp.arange(BD, dtype=jnp.int32)
    diag_rows = jnp.broadcast_to(jnp.arange(N_COL, dtype=jnp.int32)[None, :, None] * BD + diagonal, (N_ROW, N_COL, BD))
    diag_cols = jnp.broadcast_to(jnp.arange(N_ROW, dtype=jnp.int32)[:, None, None] * BD + diagonal, (N_ROW, N_COL, BD))
    all_rows = jnp.concatenate([diag_rows, random_rows.astype(jnp.int32)], 2)
    all_cols = jnp.concatenate([diag_cols, random_cols.astype(jnp.int32)], 2)
    return (all_rows, all_cols)


def draw_block_rows(key, part):
    return block_pattern(key)[0].astype(jnp.int32)


def draw_block_cols(key, part):
    return block_pattern(key)[1].astype(jnp.int32)


def draw_block_values(key, part):
    seeded = jax.random.fold_in(key, 11)
    noise_key, onsite_key = jax.random.split(seeded)
    shape = (N_ROW, N_COL, NBD, ORB, ORB)
    spread = 0.35 / math.sqrt(ORB * NBD / BD)
    noise = jax.random.normal(noise_key, shape, jnp.float32) * spread
    onsite = jax.random.uniform(onsite_key, (N_ROW, N_COL, BD, ORB), jnp.float32, -1.0, 1.0)
    diag_part = onsite[..., :, None] * jnp.eye(ORB, dtype=jnp.float32)
    full = noise.at[:, :, :BD].add(diag_part)
    return full.astype(jnp.bfloat16)


def draw_row_counts(key, part):
    seeded = jax.random.fold_in(key, 13)
    delta_key, pick_key, sign_key, first_key = jax.random.split(seeded, 4)
    pair_count = N_ROW * N_COL // 2
    half_blocks = BD // 2
    deltas = jax.random.randint(delta_key, (pair_count,), -half_blocks, half_blocks + 1)
    first_delta = jax.random.randint(first_key, (), 1, half_blocks + 1)
    deltas = jnp.where(jnp.arange(pair_count) == 0, first_delta, deltas)
    chosen = jax.random.randint(pick_key, (), 0, pair_count)
    sign_value = jax.random.randint(sign_key, (), 0, 2) * 2 - 1
    sign_value = jnp.where(chosen == 0, 1, sign_value)
    deltas = jnp.where(jnp.arange(pair_count) == chosen, sign_value * half_blocks, deltas)
    counts = jnp.stack([BD + deltas, BD - deltas], axis=1).reshape(-1)
    return counts.astype(jnp.int32)


def steps_of(key, shape, shards, least, high):
    def one(axis_at, blocks):
        steps = jax.random.uniform(jax.random.fold_in(jax.random.fold_in(key, 6), axis_at), (blocks,), jnp.float32, least / len(shards), high / len(shards))
        return jnp.repeat(jnp.exp(steps), shape[axis_at] // blocks).reshape((-1,) + (1,) * (len(shape) - axis_at - 1))

    gain = one(*shards[0])
    for cut in shards[1:]:
        gain = gain * one(*cut)
    return gain


def normal_values(stream_key, shape, deviation, reach, cuts=(), held_as=jnp.bfloat16):
    gain = steps_of(stream_key, shape, cuts, -0.22, 0.18) if cuts else 1.0
    drawn = jax.random.normal(stream_key, shape, jnp.float32) * deviation * gain
    return jnp.minimum(jnp.maximum(drawn, -reach), reach).astype(held_as)


def setup_inputs(seed: int = 0) -> dict:
    streams_of = jax.random.split(jax.random.key(seed), 8)
    return {
        "block_values": draw_block_values(jax.random.fold_in(streams_of[7], 71), 0),
        "block_rows": draw_block_rows(jax.random.fold_in(streams_of[7], 71), 0),
        "block_cols": draw_block_cols(jax.random.fold_in(streams_of[7], 71), 0),
        "start_vectors": normal_values(streams_of[3], (ORDER, VECS), 1.0, 6.0, ((0, 128),)),
        "center": jnp.clip(jax.random.uniform(streams_of[4], (1,), jnp.float32, -0.5, -0.1), -0.5, -0.1),
        "half_width": jnp.clip(jax.random.uniform(streams_of[5], (1,), jnp.float32, 0.9, 1.3), 0.9, 1.3),
        "row_counts": draw_row_counts(jax.random.fold_in(streams_of[7], 71), 0),
    }


def cell_images(values, row_ids, col_ids, vector_blocks, grid_row):
    def one_cell(running, cell_items):
        cell_values, cell_rows, cell_cols, grid_col = cell_items
        global_cols = ((cell_cols // BD) * N_COL + grid_col) * BD + cell_cols % BD
        picked = vector_blocks[global_cols.astype(jnp.int32)]
        images = jnp.einsum("kij,kjv->kiv", cell_values.astype(jnp.float32), picked.astype(jnp.float32))
        cell_sum = jnp.zeros((N_COL * BD, ORB, VECS), jnp.float32).at[cell_rows].add(images)
        rounded = lax.optimization_barrier(cell_sum.astype(jnp.bfloat16))
        return running + rounded.astype(jnp.float32), None

    initial = jnp.zeros((N_COL * BD, ORB, VECS), jnp.float32)
    cell_items = (values[grid_row], row_ids[grid_row], col_ids[grid_row], jnp.arange(N_COL, dtype=jnp.int32))
    running, _ = lax.scan(one_cell, initial, cell_items)
    return running


def apply_operator(values, row_ids, col_ids, vectors):
    vector_blocks = vectors.reshape(BD * N_ROW * N_COL, ORB, VECS)
    pieces = [cell_images(values, row_ids, col_ids, vector_blocks, grid_row) for grid_row in range(N_ROW)]
    return jnp.concatenate(pieces, 0).reshape(ORDER, VECS)


def reference(block_values, block_rows, block_cols, start_vectors, center, half_width, row_counts):
    source = start_vectors.astype(jnp.float32)
    first_image = apply_operator(block_values, block_rows, block_cols, start_vectors)
    first_step = ((first_image - center[0] * source) / half_width[0]).astype(jnp.bfloat16)
    second_image = apply_operator(block_values, block_rows, block_cols, first_step)
    second_step = (2.0 * (second_image - center[0] * first_step.astype(jnp.float32)) / half_width[0] - source).astype(jnp.bfloat16)
    offsets = (jnp.cumsum(row_counts) - row_counts).astype(jnp.int32)
    padded = jnp.concatenate([second_step, jnp.zeros((CAP * ORB, VECS), jnp.bfloat16)], 0)

    def take_rows(offset, count):
        selected = lax.dynamic_slice_in_dim(padded, (offset * ORB).astype(jnp.int32), CAP * ORB, 0)
        live_rows = jnp.arange(CAP * ORB, dtype=jnp.int32)[:, None] < count * ORB
        return jnp.where(live_rows, selected, jnp.zeros_like(selected))

    relaid = jax.vmap(take_rows)(offsets, row_counts)
    return relaid.reshape(N_ROW * N_COL * CAP * ORB, VECS)
```

```python
import functools

import jax
import jax.numpy as jnp
from jax import lax
from jax.experimental import pallas as pl
from jax.experimental.pallas import tpu as pltpu
from jax.sharding import PartitionSpec as P

ORB = 128
VECS = 256
BD = 13
MOVE = 6
GROUP = 16


def product_kernel(rows_ref, cols_ref, values_ref, panel_hbm, out_hbm, acc, panel, stage, panel_sem, out_sem):
    step = pl.program_id(0)
    steps = pl.num_programs(0)
    dests = acc.shape[0] // BD

    @pl.when(step == 0)
    def _():
        copy = pltpu.make_async_copy(panel_hbm, panel, panel_sem)
        copy.start()

        @pl.loop(0, acc.shape[0])
        def _(i):
            acc[i] = jnp.zeros((ORB, VECS), jnp.float32)

        copy.wait()

    for e in range(GROUP):
        row = rows_ref[step * GROUP + e]
        col = cols_ref[step * GROUP + e]
        acc[row] += jnp.dot(values_ref[e], panel[col], preferred_element_type=jnp.float32)

    @pl.when(step == steps - 1)
    def _():
        def out_copy(d, slot):
            return pltpu.make_async_copy(stage.at[slot], out_hbm.at[pl.ds(d * BD, BD)], out_sem.at[slot])

        for d in range(dests):
            slot = d % 2
            if d >= 2:
                out_copy(d - 2, slot).wait()

            @pl.loop(0, BD)
            def _(b):
                stage[slot, b] = acc[d * BD + b].astype(jnp.bfloat16)

            out_copy(d, slot).start()
        for d in range(dests - 2, dests):
            out_copy(d, d % 2).wait()


def cell_terms(values, row_ids, col_ids, panel_rows, out_blocks):
    count = values.shape[0]
    panel = panel_rows.reshape(-1, ORB, VECS)
    out = pl.pallas_call(
        product_kernel,
        out_shape=jax.ShapeDtypeStruct((out_blocks, ORB, VECS), jnp.bfloat16),
        grid_spec=pltpu.PrefetchScalarGridSpec(
            num_scalar_prefetch=2,
            grid=(count // GROUP,),
            in_specs=[
                pl.BlockSpec((GROUP, ORB, ORB), lambda s, r, c: (s, 0, 0)),
                pl.BlockSpec(memory_space=pl.ANY),
            ],
            out_specs=pl.BlockSpec(memory_space=pl.ANY),
            scratch_shapes=[
                pltpu.VMEM((out_blocks, ORB, VECS), jnp.float32),
                pltpu.VMEM(panel.shape, jnp.bfloat16),
                pltpu.VMEM((2, BD, ORB, VECS), jnp.bfloat16),
                pltpu.SemaphoreType.DMA,
                pltpu.SemaphoreType.DMA((2,)),
            ],
        ),
        compiler_params=pltpu.CompilerParams(
            dimension_semantics=("arbitrary",), vmem_limit_bytes=56 * 1024 * 1024
        ),
        name="block_products",
    )(row_ids, col_ids, values, panel)
    return out.reshape(out_blocks * ORB, VECS)


def swapped(block, axis):
    count = lax.axis_size(axis)
    return lax.ppermute(block, axis, [(i, i ^ 1) for i in range(count)])


def on_device(block_values, block_rows, block_cols, start_vectors, center, half_width, row_counts):
    values = block_values.reshape(-1, ORB, ORB)
    row_ids = block_rows.reshape(-1)
    col_ids = block_cols.reshape(-1)
    col_count = lax.axis_size("col")
    center_value = center[0]
    width_value = half_width[0]

    def image_of(vectors):
        panel_rows = lax.all_gather(vectors, "row", axis=0, tiled=True)
        terms = cell_terms(values, row_ids, col_ids, panel_rows, col_count * BD)
        return lax.psum_scatter(terms, "col", scatter_dimension=0, tiled=True).astype(jnp.float32)

    source = start_vectors.astype(jnp.float32)
    first_image = image_of(start_vectors)
    first_step = ((first_image - center_value * source) / width_value).astype(jnp.bfloat16)
    second_image = image_of(first_step)
    second = (
        2.0 * (second_image - center_value * first_step.astype(jnp.float32)) / width_value - source
    ).astype(jnp.bfloat16)
    device = lax.axis_index("row") * col_count + lax.axis_index("col")
    parity = device % 2
    even_count = row_counts[device - parity]
    own_count = row_counts[device]
    start_block = jnp.where(parity == 0, 0, even_count - (BD - MOVE))
    capacity = BD + MOVE
    leaving = lax.dynamic_slice_in_dim(second, (1 - parity) * ((BD - MOVE) * ORB), MOVE * ORB, 0)
    arriving = swapped(leaving, ("row", "col"))
    window = jnp.where(
        parity == 0, jnp.concatenate([second, arriving], 0), jnp.concatenate([arriving, second], 0)
    )
    padded = jnp.concatenate([window, jnp.zeros((2 * MOVE * ORB, VECS), jnp.bfloat16)], 0)
    selected = lax.dynamic_slice_in_dim(padded, start_block * ORB, capacity * ORB, 0)
    live_rows = jnp.arange(capacity * ORB, dtype=jnp.int32)[:, None] < own_count * ORB
    return jnp.where(live_rows, selected, jnp.zeros_like(selected))


def solution(mesh):
    placed = (
        P("row", "col", None, None, None),
        P("row", "col", None),
        P("row", "col", None),
        P(("row", "col"), None),
        P(),
        P(),
        P(),
    )
    return jax.shard_map(
        on_device, mesh=mesh, in_specs=placed, out_specs=P(("row", "col"), None), check_vma=False
    )
```

```python
import functools

import jax
import jax.numpy as jnp
from jax import lax
from jax.experimental import pallas as pl
from jax.experimental.pallas import tpu as pltpu
from jax.sharding import PartitionSpec as P

ORB = 128
VECS = 256
BD = 13
MOVE = 6
GROUP = 16


def product_kernel(rows_ref, cols_ref, values_ref, panel_hbm, out_hbm, acc, panel, stage, panel_sem, out_sem):
    step = pl.program_id(0)
    steps = pl.num_programs(0)
    dests = acc.shape[0] // BD

    @pl.when(step == 0)
    def _():
        copy = pltpu.make_async_copy(panel_hbm, panel, panel_sem)
        copy.start()

        @pl.loop(0, acc.shape[0])
        def _(i):
            acc[i] = jnp.zeros((ORB, VECS), jnp.float32)

        copy.wait()

    for e in range(GROUP):
        row = rows_ref[step * GROUP + e]
        col = cols_ref[step * GROUP + e]
        acc[row] += jnp.dot(values_ref[e], panel[col], preferred_element_type=jnp.float32)

    @pl.when(step == steps - 1)
    def _():
        def out_copy(d, slot):
            return pltpu.make_async_copy(stage.at[slot], out_hbm.at[pl.ds(d * BD, BD)], out_sem.at[slot])

        for d in range(dests):
            slot = d % 2
            if d >= 2:
                out_copy(d - 2, slot).wait()

            @pl.loop(0, BD)
            def _(b):
                stage[slot, b] = acc[d * BD + b].astype(jnp.bfloat16)

            out_copy(d, slot).start()
        for d in range(dests - 2, dests):
            out_copy(d, d % 2).wait()


def cell_terms(values, row_ids, col_ids, panel_rows, out_blocks):
    count = values.shape[0]
    panel = panel_rows.reshape(-1, ORB, VECS)
    out = pl.pallas_call(
        product_kernel,
        out_shape=jax.ShapeDtypeStruct((out_blocks, ORB, VECS), jnp.bfloat16),
        grid_spec=pltpu.PrefetchScalarGridSpec(
            num_scalar_prefetch=2,
            grid=(count // GROUP,),
            in_specs=[
                pl.BlockSpec((GROUP, ORB, ORB), lambda s, r, c: (s, 0, 0)),
                pl.BlockSpec(memory_space=pl.ANY),
            ],
            out_specs=pl.BlockSpec(memory_space=pl.ANY),
            scratch_shapes=[
                pltpu.VMEM((out_blocks, ORB, VECS), jnp.float32),
                pltpu.VMEM(panel.shape, jnp.bfloat16),
                pltpu.VMEM((2, BD, ORB, VECS), jnp.bfloat16),
                pltpu.SemaphoreType.DMA,
                pltpu.SemaphoreType.DMA((2,)),
            ],
        ),
        compiler_params=pltpu.CompilerParams(
            dimension_semantics=("arbitrary",), vmem_limit_bytes=56 * 1024 * 1024
        ),
        name="block_products",
    )(row_ids, col_ids, values, panel)
    return out.reshape(out_blocks * ORB, VECS)


MESH = pl.DeviceIdType.MESH
SIDE = 4
HALF = BD * ORB // 2
GROUPS = 4
PART = HALF // GROUPS
PART_A = (PART // 32) * 16 + (PART % 32)
PART_B = PART - PART_A
RELAY_A, RELAY_B, DIRECT_A, DIRECT_B, SUM_A, SUM_B = range(6)
STRIPE = 16


def shifted(position, by):
    return (position + by + SIDE) % SIDE


class Place:
    def __init__(self):
        self.row = lax.axis_index("row")
        self.col = lax.axis_index("col")
        self.z, self.core = self.row // 2, self.row % 2
        self.x, self.y = self.col // SIDE, self.col % SIDE

    def along(self, axis, by):
        if axis == 0:
            return (self.row, shifted(self.x, by) * SIDE + self.y)
        if axis == 1:
            return (self.row, self.x * SIDE + shifted(self.y, by))
        return (self.slot(by), self.col)

    def slot(self, by):
        return shifted(self.z, by) * 2 + self.core

    def partner(self):
        return (self.z * 2 + 1 - self.core, self.col)

    def greet(self, targets):
        barrier = pltpu.get_barrier_semaphore()
        for target in targets:
            pl.semaphore_signal(barrier, inc=1, device_id=target, device_id_type=MESH)
        pl.semaphore_wait(barrier, len(targets))


def remote(src, dst, send_sem, recv_sem, target):
    return pltpu.make_async_remote_copy(
        src_ref=src, dst_ref=dst, send_sem=send_sem, recv_sem=recv_sem, device_id=target, device_id_type=MESH
    )


def part_rows(group, kind):
    return pl.ds(pl.multiple_of(kind * HALF + group * PART, 16), PART)


def stripes(rows, body):
    @pl.loop(0, rows // STRIPE)
    def _(i):
        body(pl.multiple_of(i * STRIPE, STRIPE))


def wide(value):
    return value.astype(jnp.float32)


class Gather:
    def __init__(self, place, own, panel, send_sem, recv_sem):
        self.place, self.own, self.panel = place, own, panel
        self.send_sem, self.recv_sem = send_sem, recv_sem

    def copy(self, group, kind, index):
        place = self.place
        rows = part_rows(group, kind)
        plus, minus, partner = place.along(2, 1), place.along(2, -1), place.partner()
        mine, below, above, far = place.slot(0), place.slot(-1), place.slot(1), place.slot(2)
        own = self.own.at[rows]
        slot, target = [
            (mine, plus),
            (mine, minus),
            (mine, partner),
            (below, plus) if kind == 0 else (above, minus),
            (below, partner),
            (above, partner),
            (far, partner),
        ][index]
        source = own if index < 3 else self.panel.at[slot, rows]
        sems = (group, kind, index)
        return remote(source, self.panel.at[slot, rows], self.send_sem.at[sems], self.recv_sem.at[sems], target)

    def first(self, group):
        for index in range(3):
            for kind in range(2):
                self.copy(group, kind, index).start()

    def second(self, group):
        for kind in range(2):
            self.copy(group, kind, 0).wait_recv()
            self.copy(group, kind, 1).wait_recv()
            for index in (3, 4, 5):
                self.copy(group, kind, index).start()

    def third(self, group):
        for kind in range(2):
            self.copy(group, kind, 3).wait_recv()
            self.copy(group, kind, 6).start()

    def fourth(self, group):
        for kind in range(2):
            for index in (2, 4, 5, 6):
                self.copy(group, kind, index).wait_recv()

    def close(self, group):
        for kind in range(2):
            for index in range(7):
                self.copy(group, kind, index).wait_send()


def panel_out(panel, out_hbm, out_sem, group, kind):
    rows = part_rows(group, kind)
    return pltpu.make_async_copy(panel.at[:, rows], out_hbm.at[:, rows], out_sem.at[group, kind])


def gather_kernel(start_hbm, out_hbm, panel, load_sem, out_sem, send_sem, recv_sem):
    place = Place()
    own = panel.at[place.slot(0)]
    gather = Gather(place, own, panel, send_sem, recv_sem)
    load = pltpu.make_async_copy(start_hbm, own, load_sem)
    load.start()
    place.greet([place.along(2, 1), place.along(2, -1), place.partner()])
    load.wait()
    for it in range(GROUPS + 3):
        if it < GROUPS:
            gather.first(it)
        if 0 <= it - 1 < GROUPS:
            gather.second(it - 1)
        if 0 <= it - 2 < GROUPS:
            gather.third(it - 2)
        if 0 <= it - 3 < GROUPS:
            gather.fourth(it - 3)
            for kind in range(2):
                panel_out(panel, out_hbm, out_sem, it - 3, kind).start()
    for group in range(GROUPS):
        gather.close(group)
        for kind in range(2):
            panel_out(panel, out_hbm, out_sem, group, kind).wait()


class Reduce:
    def __init__(self, place, terms, minus_sum, plus_sum, result, far_slots, near_a, near_b, load_sem, far_sems, near_sems):
        self.place, self.terms = place, terms
        self.sums = (minus_sum, plus_sum)
        self.result, self.far_slots, self.near = result, far_slots, (near_a, near_b)
        self.load_sem, self.far_sems, self.near_sems = load_sem, far_sems, near_sems

    def position(self, axis):
        return self.place.x if axis == 0 else self.place.y

    def piece(self, group, kind, target, half):
        rows = part_rows(group, kind)
        span = pl.ds(0, SIDE) if half is None else pl.ds(2 * half, 2)
        if kind == 0:
            return self.terms.at[target, span, rows]
        return self.terms.at[span, target, rows]

    def load(self, group, kind, index):
        p = self.position(kind)
        sem = self.load_sem.at[group, kind, index]
        if index == 0:
            return pltpu.make_async_copy(self.piece(group, kind, shifted(p, -1), 0), self.sums[0].at[group, kind], sem)
        if index == 1:
            return pltpu.make_async_copy(self.piece(group, kind, shifted(p, 1), 1), self.sums[1].at[group, kind], sem)
        return pltpu.make_async_copy(self.piece(group, kind, p, None), self.result.at[group, kind], sem)

    def far(self, group, kind, index):
        p = self.position(kind)
        if index == RELAY_A:
            source, by = self.piece(group, kind, shifted(p, 2), 0), -1
        elif index == RELAY_B:
            source, by = self.piece(group, kind, shifted(p, 2), 1), 1
        elif index == DIRECT_B:
            source, by = self.piece(group, kind, shifted(p, -1), 1), -1
        elif index == DIRECT_A:
            source, by = self.piece(group, kind, shifted(p, 1), 0), 1
        elif index == SUM_A:
            source, by = self.sums[0].at[group, kind], -1
        else:
            source, by = self.sums[1].at[group, kind], 1
        sems = (group, kind, index)
        return remote(
            source,
            self.far_slots.at[sems],
            self.far_sems[0].at[sems],
            self.far_sems[1].at[sems],
            self.place.along(kind, by),
        )

    def near_piece(self, group, kind, target, half):
        rows = pl.ds(0, PART_A) if half == 0 else pl.ds(PART_A, PART_B)
        return self.result.at[group, kind, target, rows]

    def near_copy(self, group, kind, index):
        axis = 1 - kind
        p = self.position(axis)
        half, by, to = {
            RELAY_A: (0, -1, 2),
            RELAY_B: (1, 1, 2),
            DIRECT_B: (1, -1, -1),
            DIRECT_A: (0, 1, 1),
            SUM_A: (0, -1, -1),
            SUM_B: (1, 1, 1),
        }[index]
        source = self.near_piece(group, kind, shifted(p, to), half)
        sems = (group, kind, index)
        return remote(
            source,
            self.near[half].at[group, kind, index // 2],
            self.near_sems[0].at[sems],
            self.near_sems[1].at[sems],
            self.place.along(axis, by),
        )

    def neighbours(self):
        return [self.place.along(axis, by) for axis in (0, 1) for by in (1, -1)]

    def loads(self, group):
        for kind in range(2):
            for index in range(3):
                self.load(group, kind, index).start()

    def far_start(self, group):
        for index in (RELAY_A, RELAY_B, DIRECT_A, DIRECT_B):
            for kind in range(2):
                self.far(group, kind, index).start()

    def far_relay(self, group):
        for kind in range(2):
            for side, (arrived, leaving) in enumerate(((RELAY_A, SUM_A), (RELAY_B, SUM_B))):
                self.load(group, kind, side).wait()
                self.far(group, kind, arrived).wait_recv()
                total = self.sums[side]

                def body(at, total=total, kind=kind, arrived=arrived):
                    rows = pl.ds(at, STRIPE)
                    value = wide(total[group, kind, :, rows]) + wide(self.far_slots[group, kind, arrived, :, rows])
                    total[group, kind, :, rows] = value.astype(jnp.bfloat16)

                stripes(PART, body)
                self.far(group, kind, leaving).start()

    def far_total(self, group):
        for kind in range(2):
            self.load(group, kind, 2).wait()
            for index in (DIRECT_A, DIRECT_B, SUM_A, SUM_B):
                self.far(group, kind, index).wait_recv()

            def body(at, kind=kind):
                rows = pl.ds(at, STRIPE)
                for half, (one, two) in enumerate(((DIRECT_A, SUM_A), (DIRECT_B, SUM_B))):
                    own = pl.ds(2 * half, 2)
                    value = (
                        wide(self.result[group, kind, own, rows])
                        + wide(self.far_slots[group, kind, one, :, rows])
                        + wide(self.far_slots[group, kind, two, :, rows])
                    )
                    self.result[group, kind, own, rows] = value.astype(jnp.bfloat16)

            stripes(PART, body)
            for index in (RELAY_A, RELAY_B, DIRECT_A, DIRECT_B):
                self.near_copy(group, kind, index).start()

    def near_relay(self, group):
        for kind in range(2):
            p = self.position(1 - kind)
            for half, (arrived, leaving, to) in enumerate(((RELAY_A, SUM_A, -1), (RELAY_B, SUM_B, 1))):
                self.near_copy(group, kind, arrived).wait_recv()
                first = half * PART_A
                target = shifted(p, to)
                slots = self.near[half]

                def body(at, kind=kind, first=first, target=target, slots=slots):
                    rows = pl.ds(first + at, STRIPE)
                    value = wide(self.result[group, kind, target, rows]) + wide(slots[group, kind, 0, pl.ds(at, STRIPE)])
                    self.result[group, kind, target, rows] = value.astype(jnp.bfloat16)

                stripes((PART_A, PART_B)[half], body)
                self.near_copy(group, kind, leaving).start()

    def near_total(self, group, finish):
        for kind in range(2):
            p = self.position(1 - kind)
            for half, (one, two) in enumerate(((DIRECT_A, SUM_A), (DIRECT_B, SUM_B))):
                self.near_copy(group, kind, one).wait_recv()
                self.near_copy(group, kind, two).wait_recv()
                first = half * PART_A
                slots = self.near[half]
                base = kind * HALF + group * PART + first

                def body(at, kind=kind, first=first, slots=slots, base=base):
                    here = pl.ds(at, STRIPE)
                    value = (
                        wide(self.result[group, kind, p, pl.ds(first + at, STRIPE)])
                        + wide(slots[group, kind, 1, here])
                        + wide(slots[group, kind, 2, here])
                    )
                    finish(pl.ds(pl.multiple_of(base + at, STRIPE), STRIPE), value)

                stripes((PART_A, PART_B)[half], body)

    def close(self, group):
        for kind in range(2):
            for index in range(6):
                self.far(group, kind, index).wait_send()
                self.near_copy(group, kind, index).wait_send()


def first_kernel(center, width, terms, start_hbm, out_hbm, panel, source, source_sem, out_sem, gather_send, gather_recv, *scratch):
    place = Place()
    own = panel.at[place.slot(0)]
    gather = Gather(place, own, panel, gather_send, gather_recv)
    reduce = reducer(place, terms, scratch)
    load = pltpu.make_async_copy(start_hbm, source, source_sem)
    for group in range(GROUPS):
        reduce.loads(group)
    load.start()
    place.greet(reduce.neighbours() + [place.along(2, 1), place.along(2, -1), place.partner()])
    mine = place.slot(0)

    def finish(rows, image):
        value = (image - center[0] * wide(source[rows])) / width[0]
        panel[mine, rows] = value.astype(jnp.bfloat16)

    def opened(group):
        if group == 0:
            load.wait()
        reduce.near_total(group, finish)
        gather.first(group)

    def landed(group):
        gather.fourth(group)
        for kind in range(2):
            panel_out(panel, out_hbm, out_sem, group, kind).start()

    stages = [reduce.far_start, reduce.far_relay, reduce.far_total, reduce.near_relay, opened, gather.second, gather.third, landed]
    run(stages)
    for group in range(GROUPS):
        reduce.close(group)
        gather.close(group)
        for kind in range(2):
            panel_out(panel, out_hbm, out_sem, group, kind).wait()


def second_kernel(center, width, terms, start_hbm, panel_hbm, out_hbm, arriving, source, first, value_out, load_sem, out_sem, swap_sem, *scratch):
    place = Place()
    reduce = reducer(place, terms, scratch)
    loads = [
        pltpu.make_async_copy(start_hbm, source, load_sem.at[0]),
        pltpu.make_async_copy(panel_hbm.at[place.slot(0)], first, load_sem.at[1]),
    ]
    for group in range(GROUPS):
        reduce.loads(group)
    for load in loads:
        load.start()
    place.greet(reduce.neighbours())
    parity = place.y % 2
    other = (place.row, place.x * SIDE + place.y + 1 - 2 * parity)

    def finish(rows, image):
        value = 2.0 * (image - center[0] * wide(first[rows])) / width[0] - wide(source[rows])
        value_out[rows] = value.astype(jnp.bfloat16)

    def swap(group):
        rows = pl.ds(pl.multiple_of((1 - parity) * HALF + group * PART, 16), PART)
        here = pl.ds(group * PART, PART)
        return remote(value_out.at[rows], arriving.at[here], swap_sem.at[0, group], swap_sem.at[1, group], other)

    def out_copy(group, kind):
        rows = part_rows(group, kind)
        return pltpu.make_async_copy(value_out.at[rows], out_hbm.at[rows], out_sem.at[group, kind])

    def opened(group):
        if group == 0:
            for load in loads:
                load.wait()
        reduce.near_total(group, finish)
        swap(group).start()
        for kind in range(2):
            out_copy(group, kind).start()

    run([reduce.far_start, reduce.far_relay, reduce.far_total, reduce.near_relay, opened])
    for group in range(GROUPS):
        reduce.close(group)
        swap(group).wait()
        for kind in range(2):
            out_copy(group, kind).wait()


def run(stages):
    for it in range(GROUPS + len(stages) - 1):
        for lag, stage in enumerate(stages):
            if 0 <= it - lag < GROUPS:
                stage(it - lag)


def reducer(place, terms, scratch):
    minus_sum, plus_sum, result, far_slots, near_a, near_b, load_sem, far_s, far_r, near_s, near_r = scratch
    return Reduce(
        place, terms, minus_sum, plus_sum, result, far_slots, near_a, near_b, load_sem, (far_s, far_r), (near_s, near_r)
    )


def reduce_scratch():
    bf16 = jnp.bfloat16
    dma = pltpu.SemaphoreType.DMA
    return [
        pltpu.VMEM((GROUPS, 2, 2, PART, VECS), bf16),
        pltpu.VMEM((GROUPS, 2, 2, PART, VECS), bf16),
        pltpu.VMEM((GROUPS, 2, SIDE, PART, VECS), bf16),
        pltpu.VMEM((GROUPS, 2, 6, 2, PART, VECS), bf16),
        pltpu.VMEM((GROUPS, 2, 3, PART_A, VECS), bf16),
        pltpu.VMEM((GROUPS, 2, 3, PART_B, VECS), bf16),
        dma((GROUPS, 2, 3)),
        dma((GROUPS, 2, 6)),
        dma((GROUPS, 2, 6)),
        dma((GROUPS, 2, 6)),
        dma((GROUPS, 2, 6)),
    ]


ROWS = BD * ORB
ANY = pl.BlockSpec(memory_space=pl.ANY)
SCALAR = pl.BlockSpec(memory_space=pltpu.SMEM)


def comm_call(kernel, name, collective_id, in_specs, out_shape, scratch):
    return pl.pallas_call(
        kernel,
        out_shape=out_shape,
        in_specs=in_specs,
        out_specs=jax.tree.map(lambda _: ANY, out_shape),
        scratch_shapes=scratch,
        compiler_params=pltpu.CompilerParams(
            collective_id=collective_id, has_side_effects=True, vmem_limit_bytes=48 * 1024 * 1024
        ),
        name=name,
    )


def panel_shape(row_count):
    return jax.ShapeDtypeStruct((row_count, ROWS, VECS), jnp.bfloat16)


def gather_scratch():
    dma = pltpu.SemaphoreType.DMA
    return [dma((GROUPS, 2)), dma((GROUPS, 2, 7)), dma((GROUPS, 2, 7))]


def gathered(start, row_count):
    return comm_call(
        gather_kernel,
        "gather_rows",
        0,
        [ANY],
        panel_shape(row_count),
        [pltpu.VMEM((row_count, ROWS, VECS), jnp.bfloat16), pltpu.SemaphoreType.DMA] + gather_scratch(),
    )(start)


def first_of(center, width, terms, start, row_count):
    return comm_call(
        first_kernel,
        "reduce_and_gather",
        1,
        [SCALAR, SCALAR, ANY, ANY],
        panel_shape(row_count),
        [
            pltpu.VMEM((row_count, ROWS, VECS), jnp.bfloat16),
            pltpu.VMEM((ROWS, VECS), jnp.bfloat16),
            pltpu.SemaphoreType.DMA,
        ]
        + gather_scratch()
        + reduce_scratch(),
    )(center, width, terms.reshape(SIDE, SIDE, ROWS, VECS), start)


def second_of(center, width, terms, start, panel):
    dma = pltpu.SemaphoreType.DMA
    return comm_call(
        second_kernel,
        "reduce_and_swap",
        2,
        [SCALAR, SCALAR, ANY, ANY, ANY],
        (
            jax.ShapeDtypeStruct((ROWS, VECS), jnp.bfloat16),
            jax.ShapeDtypeStruct((HALF, VECS), jnp.bfloat16),
        ),
        [pltpu.VMEM((ROWS, VECS), jnp.bfloat16)] * 3
        + [dma((2,)), dma((GROUPS, 2)), dma((2, GROUPS))]
        + reduce_scratch(),
    )(center, width, terms.reshape(SIDE, SIDE, ROWS, VECS), start, panel)


def on_device(block_values, block_rows, block_cols, start_vectors, center, half_width, row_counts):
    values = block_values.reshape(-1, ORB, ORB)
    row_ids = block_rows.reshape(-1)
    col_ids = block_cols.reshape(-1)
    col_count = lax.axis_size("col")
    row_count = lax.axis_size("row")
    out_blocks = col_count * BD

    panel = gathered(start_vectors, row_count)
    terms = cell_terms(values, row_ids, col_ids, panel, out_blocks)
    panel = first_of(center, half_width, terms, start_vectors, row_count)
    terms = cell_terms(values, row_ids, col_ids, panel, out_blocks)
    second, arriving = second_of(center, half_width, terms, start_vectors, panel)

    device = lax.axis_index("row") * col_count + lax.axis_index("col")
    parity = device % 2
    even_count = row_counts[device - parity]
    own_count = row_counts[device]
    start_row = jnp.where(parity == 0, 0, even_count * ORB - HALF)
    capacity = (BD + MOVE) * ORB
    window = jnp.where(
        parity == 0, jnp.concatenate([second, arriving], 0), jnp.concatenate([arriving, second], 0)
    )
    padded = jnp.concatenate([window, jnp.zeros((capacity, VECS), jnp.bfloat16)], 0)
    selected = lax.dynamic_slice_in_dim(padded, start_row, capacity, 0)
    live_rows = jnp.arange(capacity, dtype=jnp.int32)[:, None] < own_count * ORB
    return jnp.where(live_rows, selected, jnp.zeros_like(selected))


def solution(mesh):
    placed = (
        P("row", "col", None, None, None),
        P("row", "col", None),
        P("row", "col", None),
        P(("row", "col"), None),
        P(),
        P(),
        P(),
    )
    return jax.shard_map(
        on_device, mesh=mesh, in_specs=placed, out_specs=P(("row", "col"), None), check_vma=False
    )
```

```python
import functools

import jax
import jax.numpy as jnp
from jax import lax
from jax.experimental import pallas as pl
from jax.experimental.pallas import tpu as pltpu
from jax.sharding import PartitionSpec as P

ORB = 128
VECS = 256
BD = 13
MOVE = 6
GROUP = 8


def product_kernel(codes_ref, values_ref, panel_ref, out_ref):
    @pl.loop(0, out_ref.shape[0])
    def _(i):
        out_ref[i] = jnp.zeros((ORB, VECS), jnp.bfloat16)

    def group(step, carry):
        before, total = carry
        for e in range(GROUP):
            code = codes_ref[step * GROUP + e]
            row, col, entry = code >> 15, (code >> 8) & 127, code & 255
            product = jnp.dot(values_ref[entry], panel_ref[col], preferred_element_type=jnp.float32)
            total = jnp.where(row == before, total, 0.0) + product
            out_ref[row] = total.astype(jnp.bfloat16)
            before = row
        return before, total

    lax.fori_loop(
        0, values_ref.shape[0] // GROUP, group, (jnp.int32(-1), jnp.zeros((ORB, VECS), jnp.float32))
    )


def entry_codes(row_ids, col_ids):
    count = row_ids.shape[0]
    codes = (row_ids * 128 + col_ids) * 256 + jnp.arange(count, dtype=jnp.int32)
    rank = jnp.sum((codes[None, :] < codes[:, None]).astype(jnp.int32), 1)
    here = rank[:, None] == jnp.arange(count, dtype=jnp.int32)[None, :]
    return jnp.sum(jnp.where(here, codes[:, None], 0), 0)


def cell_terms(codes, values, panel_rows, out_blocks):
    panel = panel_rows.reshape(-1, ORB, VECS)
    vmem = pl.BlockSpec(memory_space=pltpu.VMEM)
    return pl.pallas_call(
        product_kernel,
        out_shape=jax.ShapeDtypeStruct((out_blocks, ORB, VECS), jnp.bfloat16),
        in_specs=[pl.BlockSpec(memory_space=pltpu.SMEM), vmem, vmem],
        out_specs=vmem,
        compiler_params=pltpu.CompilerParams(vmem_limit_bytes=PRODUCT_LIMIT * 1024 * 1024),
        name="block_products",
    )(codes, values, panel)


PRODUCT_LIMIT = 10
MESH = pl.DeviceIdType.MESH
SIDE = 4
HALF = BD * ORB // 2
ROWS = BD * ORB
GATHER_PARTS = (416, 416)
FIRST_PARTS = (160, 176, 144, 112, 96, 80, 64)
SECOND_PARTS = (208, 352, 272)
RELAY_A, RELAY_B, DIRECT_A, DIRECT_B, SUM_A, SUM_B = range(6)
FIRST_ORDER = (
    0, 1, 32, 33, 2, 3, 64, 65, 34, 35, 66, 67, 96, 97, 4, 5, 98, 128, 129, 99,
    36, 37, 68, 161, 193, 130, 131, 160, 192, 69, 225, 6, 7, 224, 162, 194, 38, 39, 257, 100,
    256, 163, 195, 226, 101, 70, 71, 227, 8, 9, 133, 132, 258, 40, 41, 259, 102, 103, 72, 164,
    196, 165, 197, 73, 10, 135, 134, 228, 11, 42, 43, 12, 229, 13, 104, 166, 198, 260, 105, 261,
    167, 199, 74, 230, 75, 44, 45, 76, 231, 136, 137, 77, 262, 106, 263, 107, 168, 200, 108, 169,
    201, 138, 139, 109, 232, 140, 170, 202, 233, 171, 203, 141, 172, 204, 264, 234, 173, 205, 265, 235,
    236, 266, 237, 267, 268, 269,
)
SECOND_ORDER = (
    0, 1, 32, 33, 2, 3, 34, 35, 64, 65, 4, 5, 66, 67, 96, 97, 36, 37, 68, 69,
    98, 128, 129, 99, 100, 161, 130, 131, 160, 101, 163, 132, 133, 162, 165, 164,
)
STRIPE = 16


def shifted(position, by):
    return (position + by + SIDE) % SIDE


class Place:
    def __init__(self):
        self.row = lax.axis_index("row")
        self.col = lax.axis_index("col")
        self.z, self.core = self.row // 2, self.row % 2
        self.x, self.y = self.col // SIDE, self.col % SIDE

    def along(self, axis, by):
        if axis == 0:
            return (self.row, shifted(self.x, by) * SIDE + self.y)
        if axis == 1:
            return (self.row, self.x * SIDE + shifted(self.y, by))
        return (self.slot(by), self.col)

    def slot(self, by):
        return shifted(self.z, by) * 2 + self.core

    def partner(self):
        return (self.z * 2 + 1 - self.core, self.col)

    def greet(self, targets):
        barrier = pltpu.get_barrier_semaphore()
        for target in targets:
            pl.semaphore_signal(barrier, inc=1, device_id=target, device_id_type=MESH)
        pl.semaphore_wait(barrier, len(targets))


def remote(src, dst, send_sem, recv_sem, target):
    return pltpu.make_async_remote_copy(
        src_ref=src, dst_ref=dst, send_sem=send_sem, recv_sem=recv_sem, device_id=target, device_id_type=MESH
    )


class Parts:
    def __init__(self, sizes):
        self.sizes = sizes
        self.count = len(sizes)

    def low(self, group):
        return sum(self.sizes[:group])

    def near(self, group, half):
        size = self.sizes[group]
        first = size // 32 * 16 + size % 32
        return (self.low(group), first) if half == 0 else (self.low(group) + first, size - first)

    def rows(self, group):
        return pl.ds(self.low(group), self.sizes[group])

    def own(self, group, kind):
        return pl.ds(kind * HALF + self.low(group), self.sizes[group])

    def run(self, stages, order):
        for code in order:
            stages[code // 32](code % 32 // 2, code % 2)


def stripes(low, rows, body):
    @pl.loop(0, rows // STRIPE)
    def _(i):
        body(pl.multiple_of(low + i * STRIPE, STRIPE))


def wide(value):
    return value.astype(jnp.float32)


class Gather:
    def __init__(self, place, parts, panel, send_sem, recv_sem):
        self.place, self.parts, self.panel = place, parts, panel
        self.send_sem, self.recv_sem = send_sem, recv_sem

    def copy(self, group, kind, index):
        place = self.place
        rows = self.parts.own(group, kind)
        plus, minus, partner = place.along(2, 1), place.along(2, -1), place.partner()
        mine, below, above, far = place.slot(0), place.slot(-1), place.slot(1), place.slot(2)
        slot, target = [
            (mine, plus),
            (mine, minus),
            (mine, partner),
            (below, plus) if kind == 0 else (above, minus),
            (below, partner),
            (above, partner),
            (far, partner),
        ][index]
        block = self.panel.at[slot, rows]
        sems = (group, kind, index)
        return remote(block, block, self.send_sem.at[sems], self.recv_sem.at[sems], target)

    def neighbours(self):
        return [self.place.along(2, 1), self.place.along(2, -1), self.place.partner()]

    def first(self, group, kind):
        for index in range(3):
            self.copy(group, kind, index).start()

    def second(self, group, kind):
        self.copy(group, kind, kind).wait_recv()
        self.copy(group, kind, 3).start()
        self.copy(group, kind, 4 + kind).start()
        self.copy(group, kind, 1 - kind).wait_recv()
        self.copy(group, kind, 5 - kind).start()

    def third(self, group, kind):
        self.copy(group, kind, 3).wait_recv()
        self.copy(group, kind, 6).start()

    def close(self, group):
        for kind in range(2):
            for index in (2, 4, 5, 6):
                self.copy(group, kind, index).wait_recv()
            for index in range(7):
                self.copy(group, kind, index).wait_send()


def gather_kernel(start_ref, values_hbm, panel, values, load_sem, send_sem, recv_sem):
    place = Place()
    gather = Gather(place, Parts(GATHER_PARTS), panel, send_sem, recv_sem)
    load = pltpu.make_async_copy(start_ref, panel.at[place.slot(0)], load_sem.at[0])
    values_load = pltpu.make_async_copy(values_hbm, values, load_sem.at[1])
    load.start()
    place.greet(gather.neighbours())
    load.wait()
    for group in range(gather.parts.count):
        for kind in range(2):
            gather.first(group, kind)
        if group == 0:
            values_load.start()
    for group in range(gather.parts.count + 1):
        for kind in range(2):
            if group < gather.parts.count:
                gather.second(group, kind)
            if group > 0:
                gather.third(group - 1, kind)
    for group in range(gather.parts.count):
        gather.close(group)
    values_load.wait()


class Reduce:
    def __init__(self, place, parts, terms, sums, result, far_slots, near_slots, far_send, far_recv, near_send, near_recv):
        self.place, self.parts, self.terms = place, parts, terms
        self.sums, self.result, self.far_slots, self.near_slots = sums, result, far_slots, near_slots
        self.far_sems, self.near_sems = (far_send, far_recv), (near_send, near_recv)

    def position(self, axis):
        return self.place.x if axis == 0 else self.place.y

    def piece(self, kind, target, half, rows):
        span = pl.ds(2 * half, 2)
        return (target, span, rows) if kind == 0 else (span, target, rows)

    def far(self, group, kind, index):
        p = self.position(kind)
        rows, own = self.parts.rows(group), self.parts.own(group, kind)
        by = -1 if index in (RELAY_A, DIRECT_B, SUM_A) else 1
        if index in (RELAY_A, RELAY_B):
            source = self.terms.at[self.piece(kind, shifted(p, 2), index - RELAY_A, own)]
        elif index == DIRECT_A:
            source = self.terms.at[self.piece(kind, shifted(p, 1), 0, own)]
        elif index == DIRECT_B:
            source = self.terms.at[self.piece(kind, shifted(p, -1), 1, own)]
        else:
            source = self.sums.at[index - SUM_A, kind, :, rows]
        sems = (group, kind, index)
        return remote(
            source,
            self.far_slots.at[kind, index, :, rows],
            self.far_sems[0].at[sems],
            self.far_sems[1].at[sems],
            self.place.along(kind, by),
        )

    def near_copy(self, group, kind, index):
        axis = 1 - kind
        p = self.position(axis)
        half, by, to = {
            RELAY_A: (0, -1, 2),
            RELAY_B: (1, 1, 2),
            DIRECT_B: (1, -1, -1),
            DIRECT_A: (0, 1, 1),
            SUM_A: (0, -1, -1),
            SUM_B: (1, 1, 1),
        }[index]
        rows = pl.ds(*self.parts.near(group, half))
        sems = (group, kind, index)
        return remote(
            self.result.at[kind, shifted(p, to), rows],
            self.near_slots.at[kind, index // 2, rows],
            self.near_sems[0].at[sems],
            self.near_sems[1].at[sems],
            self.place.along(axis, by),
        )

    def neighbours(self):
        return [self.place.along(axis, by) for axis in (0, 1) for by in (1, -1)]

    def far_relays(self, group, kind):
        self.far(group, kind, RELAY_A).start()
        self.far(group, kind, RELAY_B).start()

    def far_directs(self, group, kind):
        self.far(group, kind, DIRECT_A).start()
        self.far(group, kind, DIRECT_B).start()

    def far_relay(self, group, kind):
        p = self.position(kind)
        for side, (arrived, leaving, to) in enumerate(((RELAY_A, SUM_A, -1), (RELAY_B, SUM_B, 1))):
            self.far(group, kind, arrived).wait_recv()
            target = shifted(p, to)

            def body(at, side=side, arrived=arrived, target=target):
                rows = pl.ds(at, STRIPE)
                own = pl.ds(kind * HALF + at, STRIPE)
                value = wide(self.terms[self.piece(kind, target, side, own)]) + wide(
                    self.far_slots[kind, arrived, :, rows]
                )
                self.sums[side, kind, :, rows] = value.astype(jnp.bfloat16)

            stripes(self.parts.low(group), self.parts.sizes[group], body)
            self.far(group, kind, leaving).start()

    def far_total(self, group, kind):
        p = self.position(kind)
        for index in (DIRECT_A, DIRECT_B, SUM_A, SUM_B):
            self.far(group, kind, index).wait_recv()

        def body(at):
            rows = pl.ds(at, STRIPE)
            own = pl.ds(kind * HALF + at, STRIPE)
            for half, (one, two) in enumerate(((DIRECT_A, SUM_A), (DIRECT_B, SUM_B))):
                value = (
                    wide(self.terms[self.piece(kind, p, half, own)])
                    + wide(self.far_slots[kind, one, :, rows])
                    + wide(self.far_slots[kind, two, :, rows])
                )
                self.result[kind, pl.ds(2 * half, 2), rows] = value.astype(jnp.bfloat16)

        stripes(self.parts.low(group), self.parts.sizes[group], body)
        for index in (RELAY_A, RELAY_B, DIRECT_A, DIRECT_B):
            self.near_copy(group, kind, index).start()

    def near_relay(self, group, kind):
        p = self.position(1 - kind)
        for half, (arrived, leaving, to) in enumerate(((RELAY_A, SUM_A, -1), (RELAY_B, SUM_B, 1))):
            self.near_copy(group, kind, arrived).wait_recv()
            target = shifted(p, to)

            def body(at, target=target):
                rows = pl.ds(at, STRIPE)
                value = wide(self.result[kind, target, rows]) + wide(self.near_slots[kind, 0, rows])
                self.result[kind, target, rows] = value.astype(jnp.bfloat16)

            stripes(*self.parts.near(group, half), body)
            self.near_copy(group, kind, leaving).start()

    def near_total(self, group, kind, finish):
        p = self.position(1 - kind)
        for half, (one, two) in enumerate(((DIRECT_A, SUM_A), (DIRECT_B, SUM_B))):
            self.near_copy(group, kind, one).wait_recv()
            self.near_copy(group, kind, two).wait_recv()

            def body(at):
                rows = pl.ds(at, STRIPE)
                value = (
                    wide(self.result[kind, p, rows])
                    + wide(self.near_slots[kind, 1, rows])
                    + wide(self.near_slots[kind, 2, rows])
                )
                finish(pl.ds(kind * HALF + at, STRIPE), value)

            stripes(*self.parts.near(group, half), body)

    def close(self, group):
        for kind in range(2):
            for index in range(6):
                self.far(group, kind, index).wait_send()
                self.near_copy(group, kind, index).wait_send()


def first_kernel(center, width, terms, source, panel, gather_send, gather_recv, *scratch):
    place = Place()
    parts = Parts(FIRST_PARTS)
    gather = Gather(place, parts, panel, gather_send, gather_recv)
    reduce = Reduce(place, parts, terms, *scratch)
    place.greet(reduce.neighbours() + gather.neighbours())
    mine = place.slot(0)

    def finish(rows, image):
        value = (image - center[0] * wide(source[rows])) / width[0]
        panel[mine, rows] = value.astype(jnp.bfloat16)

    def opened(group, kind):
        reduce.near_total(group, kind, finish)

    parts.run(
        [
            reduce.far_relays,
            reduce.far_directs,
            reduce.far_relay,
            reduce.far_total,
            reduce.near_relay,
            opened,
            gather.first,
            gather.second,
            gather.third,
        ],
        FIRST_ORDER,
    )
    for group in range(parts.count):
        reduce.close(group)
        gather.close(group)


def second_kernel(center, width, terms, source, panel, out, arriving, swap_sem, *scratch):
    place = Place()
    parts = Parts(SECOND_PARTS)
    reduce = Reduce(place, parts, terms, *scratch)
    place.greet(reduce.neighbours())
    parity = place.y % 2
    other = (place.row, place.x * SIDE + place.y + 1 - 2 * parity)
    mine = place.slot(0)

    def finish(rows, image):
        value = 2.0 * (image - center[0] * wide(panel[mine, rows])) / width[0] - wide(source[rows])
        out[rows] = value.astype(jnp.bfloat16)

    def swap(group):
        rows = pl.ds(pl.multiple_of((1 - parity) * HALF + parts.low(group), 16), parts.sizes[group])
        return remote(out.at[rows], arriving.at[parts.rows(group)], swap_sem.at[0, group], swap_sem.at[1, group], other)

    opened_halves = set()

    def opened(group, kind):
        reduce.near_total(group, kind, finish)
        opened_halves.add((group, kind))
        if (group, 1 - kind) in opened_halves:
            swap(group).start()

    parts.run(
        [
            reduce.far_relays,
            reduce.far_directs,
            reduce.far_relay,
            reduce.far_total,
            reduce.near_relay,
            opened,
        ],
        SECOND_ORDER,
    )
    for group in range(parts.count):
        reduce.close(group)
        swap(group).wait()


def reduce_scratch(count):
    bf16 = jnp.bfloat16
    dma = pltpu.SemaphoreType.DMA
    return [
        pltpu.VMEM((2, 2, 2, HALF, VECS), bf16),
        pltpu.VMEM((2, SIDE, HALF, VECS), bf16),
        pltpu.VMEM((2, 6, 2, HALF, VECS), bf16),
        pltpu.VMEM((2, 3, HALF, VECS), bf16),
        dma((count, 2, 6)),
        dma((count, 2, 6)),
        dma((count, 2, 6)),
        dma((count, 2, 6)),
    ]


HBM = pl.BlockSpec(memory_space=pltpu.HBM)
VMEM = pl.BlockSpec(memory_space=pltpu.VMEM)
SCALAR = pl.BlockSpec(memory_space=pltpu.SMEM)


def comm_call(kernel, name, collective_id, limit, in_specs, out_shape, scratch):
    return pl.pallas_call(
        kernel,
        out_shape=out_shape,
        in_specs=in_specs,
        out_specs=jax.tree.map(lambda _: VMEM, out_shape),
        scratch_shapes=scratch,
        compiler_params=pltpu.CompilerParams(
            collective_id=collective_id, has_side_effects=True, vmem_limit_bytes=limit * 1024 * 1024
        ),
        name=name,
    )


def panel_shape(row_count):
    return jax.ShapeDtypeStruct((row_count, ROWS, VECS), jnp.bfloat16)


def gather_scratch(count):
    dma = pltpu.SemaphoreType.DMA
    return [dma((count, 2, 7)), dma((count, 2, 7))]


def gathered(start, values, row_count):
    return comm_call(
        gather_kernel,
        "gather_rows",
        0,
        LIMITS[0],
        [HBM, HBM],
        (panel_shape(row_count), jax.ShapeDtypeStruct(values.shape, values.dtype)),
        [pltpu.SemaphoreType.DMA((2,))] + gather_scratch(len(GATHER_PARTS)),
    )(start, values)


def first_of(center, width, terms, start, row_count):
    count = len(FIRST_PARTS)
    return comm_call(
        first_kernel,
        "reduce_and_gather",
        1,
        LIMITS[1],
        [SCALAR, SCALAR, VMEM, VMEM],
        panel_shape(row_count),
        gather_scratch(count) + reduce_scratch(count),
    )(center, width, terms.reshape(SIDE, SIDE, ROWS, VECS), start)


def second_of(center, width, terms, start, panel):
    count = len(SECOND_PARTS)
    return comm_call(
        second_kernel,
        "reduce_and_swap",
        2,
        LIMITS[2],
        [SCALAR, SCALAR, VMEM, VMEM, VMEM],
        (
            jax.ShapeDtypeStruct((ROWS, VECS), jnp.bfloat16),
            jax.ShapeDtypeStruct((HALF, VECS), jnp.bfloat16),
        ),
        [pltpu.SemaphoreType.DMA((2, count))] + reduce_scratch(count),
    )(center, width, terms.reshape(SIDE, SIDE, ROWS, VECS), start, panel)


LIMITS = (4, 22, 22)


def on_device(block_values, block_rows, block_cols, start_vectors, center, half_width, row_counts):
    values = block_values.reshape(-1, ORB, ORB)
    codes = entry_codes(block_rows.reshape(-1), block_cols.reshape(-1))
    col_count = lax.axis_size("col")
    row_count = lax.axis_size("row")
    out_blocks = col_count * BD

    panel, values = gathered(
        pltpu.with_memory_space_constraint(start_vectors, pltpu.HBM),
        pltpu.with_memory_space_constraint(values, pltpu.HBM),
        row_count,
    )
    terms = cell_terms(codes, values, panel, out_blocks)
    panel = first_of(center, half_width, terms, start_vectors, row_count)
    terms = cell_terms(codes, values, panel, out_blocks)
    second, arriving = second_of(center, half_width, terms, start_vectors, panel)

    device = lax.axis_index("row") * col_count + lax.axis_index("col")
    parity = device % 2
    even_count = row_counts[device - parity]
    own_count = row_counts[device]
    start_row = jnp.where(parity == 0, 0, even_count * ORB - HALF)
    capacity = (BD + MOVE) * ORB
    window = jnp.where(
        parity == 0, jnp.concatenate([second, arriving], 0), jnp.concatenate([arriving, second], 0)
    )
    padded = jnp.concatenate([window, jnp.zeros((capacity, VECS), jnp.bfloat16)], 0)
    selected = lax.dynamic_slice_in_dim(padded, start_row, capacity, 0)
    live_rows = jnp.arange(capacity, dtype=jnp.int32)[:, None] < own_count * ORB
    return jnp.where(live_rows, selected, jnp.zeros_like(selected))


def solution(mesh):
    placed = (
        P("row", "col", None, None, None),
        P("row", "col", None),
        P("row", "col", None),
        P(("row", "col"), None),
        P(),
        P(),
        P(),
    )
    return jax.shard_map(
        on_device, mesh=mesh, in_specs=placed, out_specs=P(("row", "col"), None), check_vma=False
    )
```

```python
import functools

import jax
import jax.numpy as jnp
from jax import lax
from jax.experimental import pallas as pl
from jax.experimental.pallas import tpu as pltpu
from jax.sharding import PartitionSpec as P

ORB = 128
VECS = 256
BD = 13
MOVE = 6
GROUP = 64


def product_kernel(codes_ref, values_ref, panel_ref, out_ref):
    @pl.loop(0, out_ref.shape[0])
    def _(i):
        out_ref[i] = jnp.zeros((ORB, VECS), jnp.bfloat16)

    def group(step, carry):
        before, total = carry
        for e in range(GROUP):
            code = codes_ref[0, step * GROUP + e]
            row, col, entry = code >> 15, (code >> 8) & 127, code & 255
            product = jnp.dot(values_ref[entry], panel_ref[col], preferred_element_type=jnp.float32)
            total = jnp.where(row == before, total, 0.0) + product
            out_ref[row] = total.astype(jnp.bfloat16)
            before = row
        return before, total

    lax.fori_loop(
        0, values_ref.shape[0] // GROUP, group, (jnp.int32(-1), jnp.zeros((ORB, VECS), jnp.float32))
    )


def cell_terms(codes, values, panel_rows, out_blocks):
    panel = panel_rows.reshape(-1, ORB, VECS)
    vmem = pl.BlockSpec(memory_space=pltpu.VMEM)
    return pl.pallas_call(
        product_kernel,
        out_shape=jax.ShapeDtypeStruct((out_blocks, ORB, VECS), jnp.bfloat16),
        in_specs=[pl.BlockSpec(memory_space=pltpu.SMEM), vmem, vmem],
        out_specs=vmem,
        compiler_params=pltpu.CompilerParams(vmem_limit_bytes=PRODUCT_LIMIT * 1024 * 1024),
        name="block_products",
    )(codes, values, panel)


PRODUCT_LIMIT = 10
MESH = pl.DeviceIdType.MESH
SIDE = 4
HALF = BD * ORB // 2
ROWS = BD * ORB
GATHER_PARTS = (416, 416)
FIRST_PARTS = (256, 256, 192, 128)
SECOND_PARTS = (448, 384)
RELAY_A, RELAY_B, DIRECT_A, DIRECT_B, SUM_A, SUM_B = range(6)
FIRST_ORDER = (
    0, 1, 32, 33, 2, 3, 64, 65, 34, 35, 66, 67, 96, 97, 4, 5, 98, 128, 129, 99,
    36, 37, 68, 69, 161, 193, 130, 131, 160, 192, 225, 6, 7, 224, 38, 39, 257, 100, 256, 101,
    162, 194, 163, 195, 70, 71, 226, 133, 132, 227, 102, 103, 258, 164, 196, 259, 165, 197, 134, 135,
    166, 198, 228, 167, 199, 229, 230, 260, 231, 261, 262, 263,
)
SECOND_ORDER = (
    0, 1, 32, 33, 2, 3, 64, 65, 34, 35, 66, 67, 96, 97, 98, 99, 128, 129, 130, 131,
    160, 161, 162, 163,
)
STRIPE = 32


def shifted(position, by):
    return (position + by + SIDE) % SIDE


class Place:
    def __init__(self):
        self.row = lax.axis_index("row")
        self.col = lax.axis_index("col")
        self.z, self.core = self.row // 2, self.row % 2
        self.x, self.y = self.col // SIDE, self.col % SIDE

    def along(self, axis, by):
        if axis == 0:
            return (self.row, shifted(self.x, by) * SIDE + self.y)
        if axis == 1:
            return (self.row, self.x * SIDE + shifted(self.y, by))
        return (self.slot(by), self.col)

    def slot(self, by):
        return shifted(self.z, by) * 2 + self.core

    def partner(self):
        return (self.z * 2 + 1 - self.core, self.col)

    def greet(self, targets):
        barrier = pltpu.get_barrier_semaphore()
        for target in targets:
            pl.semaphore_signal(barrier, inc=1, device_id=target, device_id_type=MESH)
        pl.semaphore_wait(barrier, len(targets))


def remote(src, dst, send_sem, recv_sem, target):
    return pltpu.make_async_remote_copy(
        src_ref=src, dst_ref=dst, send_sem=send_sem, recv_sem=recv_sem, device_id=target, device_id_type=MESH
    )


class Parts:
    def __init__(self, sizes):
        self.sizes = sizes
        self.count = len(sizes)

    def low(self, group):
        return sum(self.sizes[:group])

    def near(self, group, half):
        size = self.sizes[group]
        first = size // 32 * 16 + size % 32
        return (self.low(group), first) if half == 0 else (self.low(group) + first, size - first)

    def rows(self, group):
        return pl.ds(self.low(group), self.sizes[group])

    def own(self, group, kind):
        return pl.ds(kind * HALF + self.low(group), self.sizes[group])

    def run(self, stages, order):
        for code in order:
            stages[code // 32](code % 32 // 2, code % 2)


def stripes(low, rows, body):
    @pl.loop(0, rows // STRIPE)
    def _(i):
        body(pl.multiple_of(low + i * STRIPE, STRIPE))


def wide(value):
    return value.astype(jnp.float32)


class Gather:
    def __init__(self, place, parts, panel, send_sem, recv_sem, own=None):
        self.place, self.parts, self.panel, self.own = place, parts, panel, own
        self.send_sem, self.recv_sem = send_sem, recv_sem

    def copy(self, group, kind, index):
        place = self.place
        rows = self.parts.own(group, kind)
        plus, minus, partner = place.along(2, 1), place.along(2, -1), place.partner()
        mine, below, above, far = place.slot(0), place.slot(-1), place.slot(1), place.slot(2)
        slot, target = [
            (mine, plus),
            (mine, minus),
            (mine, partner),
            (below, plus) if kind == 0 else (above, minus),
            (below, partner),
            (above, partner),
            (far, partner),
        ][index]
        block = self.panel.at[slot, rows]
        sems = (group, kind, index)
        source = self.own.at[rows] if self.own is not None and index < 3 else block
        return remote(source, block, self.send_sem.at[sems], self.recv_sem.at[sems], target)

    def neighbours(self):
        return [self.place.along(2, 1), self.place.along(2, -1), self.place.partner()]

    def first(self, group, kind):
        for index in range(3):
            self.copy(group, kind, index).start()

    def second(self, group, kind):
        self.copy(group, kind, kind).wait_recv()
        self.copy(group, kind, 3).start()
        self.copy(group, kind, 4 + kind).start()
        self.copy(group, kind, 1 - kind).wait_recv()
        self.copy(group, kind, 5 - kind).start()

    def third(self, group, kind):
        self.copy(group, kind, 3).wait_recv()
        self.copy(group, kind, 6).start()

    def close(self, group):
        for kind in range(2):
            for index in (2, 4, 5, 6):
                self.copy(group, kind, index).wait_recv()
            for index in range(7):
                self.copy(group, kind, index).wait_send()


def sorted_codes(rows_ref, cols_ref):
    count = rows_ref.shape[1]
    entry = lax.broadcasted_iota(jnp.int32, (1, count), 1)
    codes = wide((rows_ref[...] * 128 + cols_ref[...]) * 256 + entry)
    across = jnp.broadcast_to(codes, (count, count))
    down = across.T
    rank = jnp.sum(jnp.where(across < down, 1.0, 0.0), axis=1, keepdims=True)
    place = wide(lax.broadcasted_iota(jnp.int32, (count, count), 1))
    return jnp.sum(jnp.where(rank == place, down, 0.0), axis=0, keepdims=True).astype(jnp.int32)


def gather_kernel(rows_ref, cols_ref, start_hbm, values_hbm, panel, values, codes, load_sem, send_sem, recv_sem):
    place = Place()
    gather = Gather(place, Parts(GATHER_PARTS), panel, send_sem, recv_sem, start_hbm)
    load = pltpu.make_async_copy(start_hbm, panel.at[place.slot(0)], load_sem.at[0])
    values_load = pltpu.make_async_copy(values_hbm, values, load_sem.at[1])
    place.greet(gather.neighbours())
    for group in range(gather.parts.count):
        for kind in range(2):
            gather.first(group, kind)
    load.start()
    values_load.start()
    codes[...] = sorted_codes(rows_ref, cols_ref)
    for group in range(gather.parts.count + 1):
        for kind in range(2):
            if group < gather.parts.count:
                gather.second(group, kind)
            if group > 0:
                gather.third(group - 1, kind)
    for group in range(gather.parts.count):
        gather.close(group)
    load.wait()
    values_load.wait()


class Reduce:
    def __init__(self, place, parts, terms, sums, result, far_slots, near_slots, far_send, far_recv, near_send, near_recv):
        self.place, self.parts, self.terms = place, parts, terms
        self.sums, self.result, self.far_slots, self.near_slots = sums, result, far_slots, near_slots
        self.far_sems, self.near_sems = (far_send, far_recv), (near_send, near_recv)

    def position(self, axis):
        return self.place.x if axis == 0 else self.place.y

    def piece(self, kind, target, half, rows):
        span = pl.ds(2 * half, 2)
        return (target, span, rows) if kind == 0 else (span, target, rows)

    def far(self, group, kind, index):
        p = self.position(kind)
        rows, own = self.parts.rows(group), self.parts.own(group, kind)
        by = -1 if index in (RELAY_A, DIRECT_B, SUM_A) else 1
        if index in (RELAY_A, RELAY_B):
            source = self.terms.at[self.piece(kind, shifted(p, 2), index - RELAY_A, own)]
        elif index == DIRECT_A:
            source = self.terms.at[self.piece(kind, shifted(p, 1), 0, own)]
        elif index == DIRECT_B:
            source = self.terms.at[self.piece(kind, shifted(p, -1), 1, own)]
        else:
            source = self.sums.at[index - SUM_A, kind, :, rows]
        sems = (group, kind, index)
        return remote(
            source,
            self.far_slots.at[kind, index, :, rows],
            self.far_sems[0].at[sems],
            self.far_sems[1].at[sems],
            self.place.along(kind, by),
        )

    def near_copy(self, group, kind, index):
        axis = 1 - kind
        p = self.position(axis)
        half, by, to = {
            RELAY_A: (0, -1, 2),
            RELAY_B: (1, 1, 2),
            DIRECT_B: (1, -1, -1),
            DIRECT_A: (0, 1, 1),
            SUM_A: (0, -1, -1),
            SUM_B: (1, 1, 1),
        }[index]
        rows = pl.ds(*self.parts.near(group, half))
        sems = (group, kind, index)
        return remote(
            self.result.at[kind, shifted(p, to), rows],
            self.near_slots.at[kind, index // 2, rows],
            self.near_sems[0].at[sems],
            self.near_sems[1].at[sems],
            self.place.along(axis, by),
        )

    def neighbours(self):
        return [self.place.along(axis, by) for axis in (0, 1) for by in (1, -1)]

    def far_relays(self, group, kind):
        self.far(group, kind, RELAY_A).start()
        self.far(group, kind, RELAY_B).start()

    def far_directs(self, group, kind):
        self.far(group, kind, DIRECT_A).start()
        self.far(group, kind, DIRECT_B).start()

    def far_relay(self, group, kind):
        p = self.position(kind)
        for side, (arrived, leaving, to) in enumerate(((RELAY_A, SUM_A, -1), (RELAY_B, SUM_B, 1))):
            self.far(group, kind, arrived).wait_recv()
            target = shifted(p, to)

            def body(at, side=side, arrived=arrived, target=target):
                rows = pl.ds(at, STRIPE)
                own = pl.ds(kind * HALF + at, STRIPE)
                self.sums[side, kind, :, rows] = (
                    self.terms[self.piece(kind, target, side, own)] + self.far_slots[kind, arrived, :, rows]
                )

            stripes(self.parts.low(group), self.parts.sizes[group], body)
            self.far(group, kind, leaving).start()

    def far_total(self, group, kind):
        p = self.position(kind)
        for index in (DIRECT_A, DIRECT_B, SUM_A, SUM_B):
            self.far(group, kind, index).wait_recv()

        def body(at):
            rows = pl.ds(at, STRIPE)
            own = pl.ds(kind * HALF + at, STRIPE)
            for half, (one, two) in enumerate(((DIRECT_A, SUM_A), (DIRECT_B, SUM_B))):
                value = (
                    wide(self.terms[self.piece(kind, p, half, own)])
                    + wide(self.far_slots[kind, one, :, rows])
                    + wide(self.far_slots[kind, two, :, rows])
                )
                self.result[kind, pl.ds(2 * half, 2), rows] = value.astype(jnp.bfloat16)

        stripes(self.parts.low(group), self.parts.sizes[group], body)
        for index in (RELAY_A, RELAY_B, DIRECT_A, DIRECT_B):
            self.near_copy(group, kind, index).start()

    def near_relay(self, group, kind):
        p = self.position(1 - kind)
        for half, (arrived, leaving, to) in enumerate(((RELAY_A, SUM_A, -1), (RELAY_B, SUM_B, 1))):
            self.near_copy(group, kind, arrived).wait_recv()
            target = shifted(p, to)

            def body(at, target=target):
                rows = pl.ds(at, STRIPE)
                self.result[kind, target, rows] += self.near_slots[kind, 0, rows]

            stripes(*self.parts.near(group, half), body)
            self.near_copy(group, kind, leaving).start()

    def near_total(self, group, kind, finish):
        p = self.position(1 - kind)
        for half, (one, two) in enumerate(((DIRECT_A, SUM_A), (DIRECT_B, SUM_B))):
            self.near_copy(group, kind, one).wait_recv()
            self.near_copy(group, kind, two).wait_recv()

            def body(at):
                rows = pl.ds(at, STRIPE)
                value = (
                    wide(self.result[kind, p, rows])
                    + wide(self.near_slots[kind, 1, rows])
                    + wide(self.near_slots[kind, 2, rows])
                )
                finish(pl.ds(kind * HALF + at, STRIPE), value)

            stripes(*self.parts.near(group, half), body)

    def close(self, group):
        for kind in range(2):
            for index in range(6):
                self.far(group, kind, index).wait_send()
                self.near_copy(group, kind, index).wait_send()


def first_kernel(center, width, terms, source, panel, gather_send, gather_recv, *scratch):
    place = Place()
    parts = Parts(FIRST_PARTS)
    gather = Gather(place, parts, panel, gather_send, gather_recv)
    reduce = Reduce(place, parts, terms, *scratch)
    place.greet(reduce.neighbours() + gather.neighbours())
    mine = place.slot(0)

    def finish(rows, image):
        value = (image - center[0] * wide(source[rows])) / width[0]
        panel[mine, rows] = value.astype(jnp.bfloat16)

    def opened(group, kind):
        reduce.near_total(group, kind, finish)

    parts.run(
        [
            reduce.far_relays,
            reduce.far_directs,
            reduce.far_relay,
            reduce.far_total,
            reduce.near_relay,
            opened,
            gather.first,
            gather.second,
            gather.third,
        ],
        FIRST_ORDER,
    )
    for group in range(parts.count):
        reduce.close(group)
        gather.close(group)


def second_kernel(center, width, terms, source, panel, out, arriving, swap_sem, *scratch):
    place = Place()
    parts = Parts(SECOND_PARTS)
    reduce = Reduce(place, parts, terms, *scratch)
    place.greet(reduce.neighbours())
    parity = place.y % 2
    other = (place.row, place.x * SIDE + place.y + 1 - 2 * parity)
    mine = place.slot(0)

    def finish(rows, image):
        value = 2.0 * (image - center[0] * wide(panel[mine, rows])) / width[0] - wide(source[rows])
        out[rows] = value.astype(jnp.bfloat16)

    def swap(group):
        rows = pl.ds(pl.multiple_of((1 - parity) * HALF + parts.low(group), 16), parts.sizes[group])
        return remote(out.at[rows], arriving.at[parts.rows(group)], swap_sem.at[0, group], swap_sem.at[1, group], other)

    opened_halves = set()

    def opened(group, kind):
        reduce.near_total(group, kind, finish)
        opened_halves.add((group, kind))
        if (group, 1 - kind) in opened_halves:
            swap(group).start()

    parts.run(
        [
            reduce.far_relays,
            reduce.far_directs,
            reduce.far_relay,
            reduce.far_total,
            reduce.near_relay,
            opened,
        ],
        SECOND_ORDER,
    )
    for group in range(parts.count):
        reduce.close(group)
        swap(group).wait()


def reduce_scratch(count):
    bf16 = jnp.bfloat16
    dma = pltpu.SemaphoreType.DMA
    return [
        pltpu.VMEM((2, 2, 2, HALF, VECS), bf16),
        pltpu.VMEM((2, SIDE, HALF, VECS), bf16),
        pltpu.VMEM((2, 6, 2, HALF, VECS), bf16),
        pltpu.VMEM((2, 3, HALF, VECS), bf16),
        dma((count, 2, 6)),
        dma((count, 2, 6)),
        dma((count, 2, 6)),
        dma((count, 2, 6)),
    ]


HBM = pl.BlockSpec(memory_space=pltpu.HBM)
VMEM = pl.BlockSpec(memory_space=pltpu.VMEM)
SCALAR = pl.BlockSpec(memory_space=pltpu.SMEM)


def comm_call(kernel, name, collective_id, limit, in_specs, out_shape, scratch):
    return pl.pallas_call(
        kernel,
        out_shape=out_shape,
        in_specs=in_specs,
        out_specs=jax.tree.map(lambda _: VMEM, out_shape),
        scratch_shapes=scratch,
        compiler_params=pltpu.CompilerParams(
            collective_id=collective_id, has_side_effects=True, vmem_limit_bytes=limit * 1024 * 1024
        ),
        name=name,
    )


def panel_shape(row_count):
    return jax.ShapeDtypeStruct((row_count, ROWS, VECS), jnp.bfloat16)


def gather_scratch(count):
    dma = pltpu.SemaphoreType.DMA
    return [dma((count, 2, 7)), dma((count, 2, 7))]


def gathered(row_ids, col_ids, start, values, row_count):
    return comm_call(
        gather_kernel,
        "gather_rows",
        0,
        LIMITS[0],
        [VMEM, VMEM, HBM, HBM],
        (
            panel_shape(row_count),
            jax.ShapeDtypeStruct(values.shape, values.dtype),
            jax.ShapeDtypeStruct(row_ids.shape, jnp.int32),
        ),
        [pltpu.SemaphoreType.DMA((2,))] + gather_scratch(len(GATHER_PARTS)),
    )(row_ids, col_ids, start, values)


def first_of(center, width, terms, start, row_count):
    count = len(FIRST_PARTS)
    return comm_call(
        first_kernel,
        "reduce_and_gather",
        1,
        LIMITS[1],
        [SCALAR, SCALAR, VMEM, VMEM],
        panel_shape(row_count),
        gather_scratch(count) + reduce_scratch(count),
    )(center, width, terms.reshape(SIDE, SIDE, ROWS, VECS), start)


def second_of(center, width, terms, start, panel):
    count = len(SECOND_PARTS)
    return comm_call(
        second_kernel,
        "reduce_and_swap",
        2,
        LIMITS[2],
        [SCALAR, SCALAR, VMEM, VMEM, VMEM],
        (
            jax.ShapeDtypeStruct((ROWS, VECS), jnp.bfloat16),
            jax.ShapeDtypeStruct((HALF, VECS), jnp.bfloat16),
        ),
        [pltpu.SemaphoreType.DMA((2, count))] + reduce_scratch(count),
    )(center, width, terms.reshape(SIDE, SIDE, ROWS, VECS), start, panel)


LIMITS = (4, 22, 22)


def on_device(block_values, block_rows, block_cols, start_vectors, center, half_width, row_counts):
    values = block_values.reshape(-1, ORB, ORB)
    row_ids = block_rows.reshape(1, -1)
    col_ids = block_cols.reshape(1, -1)
    col_count = lax.axis_size("col")
    row_count = lax.axis_size("row")
    out_blocks = col_count * BD

    panel, values, codes = gathered(
        row_ids,
        col_ids,
        pltpu.with_memory_space_constraint(start_vectors, pltpu.HBM),
        pltpu.with_memory_space_constraint(values, pltpu.HBM),
        row_count,
    )
    terms = cell_terms(codes, values, panel, out_blocks)
    panel = first_of(center, half_width, terms, start_vectors, row_count)
    terms = cell_terms(codes, values, panel, out_blocks)
    second, arriving = second_of(center, half_width, terms, start_vectors, panel)

    return placed_rows(row_counts, second, arriving)


UNIT = ORB // 2


def placing_kernel(counts_ref, second, arriving, out):
    device = lax.axis_index("row") * lax.axis_size("col") + lax.axis_index("col")
    parity = device % 2
    even_count = counts_ref[device - parity]
    live = 2 * counts_ref[device]
    first = parity * (2 * even_count - BD)

    @pl.loop(0, out.shape[0] // UNIT)
    def _(unit):
        at = first + unit
        here = pl.ds(pl.multiple_of(unit * UNIT, UNIT), UNIT)
        own_at = at - parity * BD
        other_at = at - (1 - parity) * 2 * BD
        is_own = jnp.logical_and(own_at >= 0, own_at < 2 * BD)
        is_live = unit < live

        @pl.when(jnp.logical_and(is_live, is_own))
        def _():
            out[here] = second[pl.ds(pl.multiple_of(own_at * UNIT, UNIT), UNIT)]

        @pl.when(jnp.logical_and(is_live, jnp.logical_not(is_own)))
        def _():
            out[here] = arriving[pl.ds(pl.multiple_of(other_at * UNIT, UNIT), UNIT)]

        @pl.when(jnp.logical_not(is_live))
        def _():
            out[here] = jnp.zeros((UNIT, VECS), jnp.bfloat16)


def placed_rows(row_counts, second, arriving):
    return pl.pallas_call(
        placing_kernel,
        out_shape=jax.ShapeDtypeStruct(((BD + MOVE) * ORB, VECS), jnp.bfloat16),
        in_specs=[SCALAR, VMEM, VMEM],
        out_specs=VMEM,
        compiler_params=pltpu.CompilerParams(vmem_limit_bytes=10 * 1024 * 1024),
        name="place_rows",
    )(row_counts, second, arriving)


def solution(mesh):
    placed = (
        P("row", "col", None, None, None),
        P("row", "col", None),
        P("row", "col", None),
        P(("row", "col"), None),
        P(),
        P(),
        P(),
    )
    return jax.shard_map(
        on_device, mesh=mesh, in_specs=placed, out_specs=P(("row", "col"), None), check_vma=False
    )
```

```python
import functools

import jax
import jax.numpy as jnp
from jax import lax
from jax.experimental import pallas as pl
from jax.experimental.pallas import tpu as pltpu
from jax.sharding import PartitionSpec as P

ORB = 128
VECS = 256
BD = 13
MOVE = 6
GROUP = 64


def product_kernel(codes_ref, values_ref, panel_ref, out_ref):
    @pl.loop(0, out_ref.shape[0])
    def _(i):
        out_ref[i] = jnp.zeros((ORB, VECS), jnp.bfloat16)

    def group(step, carry):
        before, total = carry
        for e in range(GROUP):
            code = codes_ref[0, step * GROUP + e]
            row, col, entry = code >> 15, (code >> 8) & 127, code & 255
            product = jnp.dot(values_ref[entry], panel_ref[col], preferred_element_type=jnp.float32)
            total = jnp.where(row == before, total, 0.0) + product
            out_ref[row] = total.astype(jnp.bfloat16)
            before = row
        return before, total

    lax.fori_loop(
        0, values_ref.shape[0] // GROUP, group, (jnp.int32(-1), jnp.zeros((ORB, VECS), jnp.float32))
    )


def cell_terms(codes, values, panel_rows, out_blocks):
    panel = panel_rows.reshape(-1, ORB, VECS)
    vmem = pl.BlockSpec(memory_space=pltpu.VMEM)
    return pl.pallas_call(
        product_kernel,
        out_shape=jax.ShapeDtypeStruct((out_blocks, ORB, VECS), jnp.bfloat16),
        in_specs=[pl.BlockSpec(memory_space=pltpu.SMEM), vmem, vmem],
        out_specs=vmem,
        compiler_params=pltpu.CompilerParams(vmem_limit_bytes=PRODUCT_LIMIT * 1024 * 1024),
        name="block_products",
    )(codes, values, panel)


PRODUCT_LIMIT = 10
MESH = pl.DeviceIdType.MESH
SIDE = 4
HALF = BD * ORB // 2
ROWS = BD * ORB
GATHER_PARTS = (832,)
FIRST_PARTS = (256, 256, 192, 128)
SECOND_PARTS = (448, 384)
RELAY_A, RELAY_B, DIRECT_A, DIRECT_B, SUM_A, SUM_B = range(6)
FIRST_ORDER = (
    0, 1, 32, 33, 2, 3, 64, 65, 34, 35, 66, 67, 96, 97, 4, 5, 98, 128, 129, 99,
    36, 37, 68, 69, 161, 193, 130, 131, 160, 192, 225, 6, 7, 224, 38, 39, 257, 100, 256, 101,
    162, 194, 163, 195, 70, 71, 226, 133, 132, 227, 102, 103, 258, 164, 196, 259, 165, 197, 134, 135,
    166, 198, 228, 167, 199, 229, 230, 260, 231, 261, 262, 263,
)
SECOND_ORDER = (
    0, 1, 32, 33, 2, 3, 64, 65, 34, 35, 66, 67, 96, 97, 98, 99, 128, 129, 130, 131,
    160, 161, 162, 163,
)
STRIPE = 32


def shifted(position, by):
    return (position + by + SIDE) % SIDE


class Place:
    def __init__(self):
        self.row = lax.axis_index("row")
        self.col = lax.axis_index("col")
        self.z, self.core = self.row // 2, self.row % 2
        self.x, self.y = self.col // SIDE, self.col % SIDE

    def along(self, axis, by):
        if axis == 0:
            return (self.row, shifted(self.x, by) * SIDE + self.y)
        if axis == 1:
            return (self.row, self.x * SIDE + shifted(self.y, by))
        return (self.slot(by), self.col)

    def slot(self, by):
        return shifted(self.z, by) * 2 + self.core

    def partner(self):
        return (self.z * 2 + 1 - self.core, self.col)

    def greet(self, targets):
        barrier = pltpu.get_barrier_semaphore()
        for target in targets:
            pl.semaphore_signal(barrier, inc=1, device_id=target, device_id_type=MESH)
        pl.semaphore_wait(barrier, len(targets))


def remote(src, dst, send_sem, recv_sem, target):
    return pltpu.make_async_remote_copy(
        src_ref=src, dst_ref=dst, send_sem=send_sem, recv_sem=recv_sem, device_id=target, device_id_type=MESH
    )


class Parts:
    def __init__(self, sizes):
        self.sizes = sizes
        self.count = len(sizes)

    def low(self, group):
        return sum(self.sizes[:group])

    def near(self, group, half):
        size = self.sizes[group]
        first = size // 32 * 16 + size % 32
        return (self.low(group), first) if half == 0 else (self.low(group) + first, size - first)

    def rows(self, group):
        return pl.ds(self.low(group), self.sizes[group])

    def own(self, group, kind):
        return pl.ds(kind * HALF + self.low(group), self.sizes[group])

    def run(self, stages, order):
        for code in order:
            stages[code // 32](code % 32 // 2, code % 2)


def stripes(low, rows, body):
    @pl.loop(0, rows // STRIPE)
    def _(i):
        body(pl.multiple_of(low + i * STRIPE, STRIPE))


def wide(value):
    return value.astype(jnp.float32)


class Gather:
    def __init__(self, place, parts, panel, send_sem, recv_sem, own=None):
        self.place, self.parts, self.panel, self.own = place, parts, panel, own
        self.send_sem, self.recv_sem = send_sem, recv_sem

    def copy(self, group, kind, index):
        place = self.place
        rows = self.parts.own(group, kind)
        plus, minus, partner = place.along(2, 1), place.along(2, -1), place.partner()
        mine, below, above, far = place.slot(0), place.slot(-1), place.slot(1), place.slot(2)
        slot, target = [
            (mine, plus),
            (mine, minus),
            (mine, partner),
            (below, plus) if kind == 0 else (above, minus),
            (below, partner),
            (above, partner),
            (far, partner),
        ][index]
        block = self.panel.at[slot, rows]
        sems = (group, kind, index)
        source = self.own.at[rows] if self.own is not None and index < 3 else block
        return remote(source, block, self.send_sem.at[sems], self.recv_sem.at[sems], target)

    def neighbours(self):
        return [self.place.along(2, 1), self.place.along(2, -1), self.place.partner()]

    def first(self, group, kind):
        for index in range(3):
            self.copy(group, kind, index).start()

    def second(self, group, kind):
        self.copy(group, kind, kind).wait_recv()
        self.copy(group, kind, 3).start()
        self.copy(group, kind, 4 + kind).start()
        self.copy(group, kind, 1 - kind).wait_recv()
        self.copy(group, kind, 5 - kind).start()

    def third(self, group, kind):
        self.copy(group, kind, 3).wait_recv()
        self.copy(group, kind, 6).start()

    def close(self, group):
        for kind in range(2):
            for index in (2, 4, 5, 6):
                self.copy(group, kind, index).wait_recv()
            for index in range(7):
                self.copy(group, kind, index).wait_send()


def sorted_codes(rows_ref, cols_ref):
    count = rows_ref.shape[1]
    entry = lax.broadcasted_iota(jnp.int32, (1, count), 1)
    codes = wide((rows_ref[...] * 128 + cols_ref[...]) * 256 + entry)
    across = jnp.broadcast_to(codes, (count, count))
    down = across.T
    rank = jnp.sum(jnp.where(across < down, 1.0, 0.0), axis=1, keepdims=True)
    place = wide(lax.broadcasted_iota(jnp.int32, (count, count), 1))
    return jnp.sum(jnp.where(rank == place, down, 0.0), axis=0, keepdims=True).astype(jnp.int32)


def gather_kernel(rows_hbm, cols_hbm, start_hbm, values_hbm, panel, values, codes, rows_ref, cols_ref, load_sem, send_sem, recv_sem):
    place = Place()
    gather = Gather(place, Parts(GATHER_PARTS), panel, send_sem, recv_sem, start_hbm)
    load = pltpu.make_async_copy(start_hbm, panel.at[place.slot(0)], load_sem.at[0])
    values_load = pltpu.make_async_copy(values_hbm, values, load_sem.at[1])
    id_loads = [
        pltpu.make_async_copy(rows_hbm, rows_ref, load_sem.at[2]),
        pltpu.make_async_copy(cols_hbm, cols_ref, load_sem.at[3]),
    ]
    for id_load in id_loads:
        id_load.start()
    place.greet(gather.neighbours())
    for group in range(gather.parts.count):
        for kind in range(2):
            gather.first(group, kind)
    load.start()
    values_load.start()
    for id_load in id_loads:
        id_load.wait()
    codes[...] = sorted_codes(rows_ref, cols_ref)
    for group in range(gather.parts.count + 1):
        for kind in range(2):
            if group < gather.parts.count:
                gather.second(group, kind)
            if group > 0:
                gather.third(group - 1, kind)
    for group in range(gather.parts.count):
        gather.close(group)
    load.wait()
    values_load.wait()


class Reduce:
    def __init__(self, place, parts, terms, sums, result, far_slots, near_slots, far_send, far_recv, near_send, near_recv):
        self.place, self.parts, self.terms = place, parts, terms
        self.sums, self.result, self.far_slots, self.near_slots = sums, result, far_slots, near_slots
        self.far_sems, self.near_sems = (far_send, far_recv), (near_send, near_recv)

    def position(self, axis):
        return self.place.x if axis == 0 else self.place.y

    def piece(self, kind, target, half, rows):
        span = pl.ds(2 * half, 2)
        return (target, span, rows) if kind == 0 else (span, target, rows)

    def far(self, group, kind, index):
        p = self.position(kind)
        rows, own = self.parts.rows(group), self.parts.own(group, kind)
        by = -1 if index in (RELAY_A, DIRECT_B, SUM_A) else 1
        if index in (RELAY_A, RELAY_B):
            source = self.terms.at[self.piece(kind, shifted(p, 2), index - RELAY_A, own)]
        elif index == DIRECT_A:
            source = self.terms.at[self.piece(kind, shifted(p, 1), 0, own)]
        elif index == DIRECT_B:
            source = self.terms.at[self.piece(kind, shifted(p, -1), 1, own)]
        else:
            source = self.sums.at[index - SUM_A, kind, :, rows]
        sems = (group, kind, index)
        return remote(
            source,
            self.far_slots.at[kind, index, :, rows],
            self.far_sems[0].at[sems],
            self.far_sems[1].at[sems],
            self.place.along(kind, by),
        )

    def near_copy(self, group, kind, index):
        axis = 1 - kind
        p = self.position(axis)
        half, by, to = {
            RELAY_A: (0, -1, 2),
            RELAY_B: (1, 1, 2),
            DIRECT_B: (1, -1, -1),
            DIRECT_A: (0, 1, 1),
            SUM_A: (0, -1, -1),
            SUM_B: (1, 1, 1),
        }[index]
        rows = pl.ds(*self.parts.near(group, half))
        sems = (group, kind, index)
        return remote(
            self.result.at[kind, shifted(p, to), rows],
            self.near_slots.at[kind, index // 2, rows],
            self.near_sems[0].at[sems],
            self.near_sems[1].at[sems],
            self.place.along(axis, by),
        )

    def neighbours(self):
        return [self.place.along(axis, by) for axis in (0, 1) for by in (1, -1)]

    def far_relays(self, group, kind):
        self.far(group, kind, RELAY_A).start()
        self.far(group, kind, RELAY_B).start()

    def far_directs(self, group, kind):
        self.far(group, kind, DIRECT_A).start()
        self.far(group, kind, DIRECT_B).start()

    def far_relay(self, group, kind):
        p = self.position(kind)
        for side, (arrived, leaving, to) in enumerate(((RELAY_A, SUM_A, -1), (RELAY_B, SUM_B, 1))):
            self.far(group, kind, arrived).wait_recv()
            target = shifted(p, to)

            def body(at, side=side, arrived=arrived, target=target):
                rows = pl.ds(at, STRIPE)
                own = pl.ds(kind * HALF + at, STRIPE)
                self.sums[side, kind, :, rows] = (
                    self.terms[self.piece(kind, target, side, own)] + self.far_slots[kind, arrived, :, rows]
                )

            stripes(self.parts.low(group), self.parts.sizes[group], body)
            self.far(group, kind, leaving).start()

    def far_total(self, group, kind):
        p = self.position(kind)
        for index in (DIRECT_A, DIRECT_B, SUM_A, SUM_B):
            self.far(group, kind, index).wait_recv()

        def body(at):
            rows = pl.ds(at, STRIPE)
            own = pl.ds(kind * HALF + at, STRIPE)
            for half, (one, two) in enumerate(((DIRECT_A, SUM_A), (DIRECT_B, SUM_B))):
                value = (
                    wide(self.terms[self.piece(kind, p, half, own)])
                    + wide(self.far_slots[kind, one, :, rows])
                    + wide(self.far_slots[kind, two, :, rows])
                )
                self.result[kind, pl.ds(2 * half, 2), rows] = value.astype(jnp.bfloat16)

        stripes(self.parts.low(group), self.parts.sizes[group], body)
        for index in (RELAY_A, RELAY_B, DIRECT_A, DIRECT_B):
            self.near_copy(group, kind, index).start()

    def near_relay(self, group, kind):
        p = self.position(1 - kind)
        for half, (arrived, leaving, to) in enumerate(((RELAY_A, SUM_A, -1), (RELAY_B, SUM_B, 1))):
            self.near_copy(group, kind, arrived).wait_recv()
            target = shifted(p, to)

            def body(at, target=target):
                rows = pl.ds(at, STRIPE)
                self.result[kind, target, rows] += self.near_slots[kind, 0, rows]

            stripes(*self.parts.near(group, half), body)
            self.near_copy(group, kind, leaving).start()

    def near_total(self, group, kind, finish):
        p = self.position(1 - kind)
        for half, (one, two) in enumerate(((DIRECT_A, SUM_A), (DIRECT_B, SUM_B))):
            self.near_copy(group, kind, one).wait_recv()
            self.near_copy(group, kind, two).wait_recv()

            def body(at):
                rows = pl.ds(at, STRIPE)
                value = (
                    wide(self.result[kind, p, rows])
                    + wide(self.near_slots[kind, 1, rows])
                    + wide(self.near_slots[kind, 2, rows])
                )
                finish(pl.ds(kind * HALF + at, STRIPE), value)

            stripes(*self.parts.near(group, half), body)

    def close(self, group):
        for kind in range(2):
            for index in range(6):
                self.far(group, kind, index).wait_send()
                self.near_copy(group, kind, index).wait_send()


def first_kernel(center, width, terms, source, panel, gather_send, gather_recv, *scratch):
    place = Place()
    parts = Parts(FIRST_PARTS)
    gather = Gather(place, parts, panel, gather_send, gather_recv)
    reduce = Reduce(place, parts, terms, *scratch)
    place.greet(reduce.neighbours() + gather.neighbours())
    mine = place.slot(0)

    def finish(rows, image):
        value = (image - center[0] * wide(source[rows])) / width[0]
        panel[mine, rows] = value.astype(jnp.bfloat16)

    def opened(group, kind):
        reduce.near_total(group, kind, finish)

    parts.run(
        [
            reduce.far_relays,
            reduce.far_directs,
            reduce.far_relay,
            reduce.far_total,
            reduce.near_relay,
            opened,
            gather.first,
            gather.second,
            gather.third,
        ],
        FIRST_ORDER,
    )
    for group in range(parts.count):
        reduce.close(group)
        gather.close(group)


def second_kernel(center, width, terms, source, panel, out, arriving, swap_sem, *scratch):
    place = Place()
    parts = Parts(SECOND_PARTS)
    reduce = Reduce(place, parts, terms, *scratch)
    place.greet(reduce.neighbours())
    parity = place.y % 2
    other = (place.row, place.x * SIDE + place.y + 1 - 2 * parity)
    mine = place.slot(0)

    def finish(rows, image):
        value = 2.0 * (image - center[0] * wide(panel[mine, rows])) / width[0] - wide(source[rows])
        out[rows] = value.astype(jnp.bfloat16)

    def swap(group):
        rows = pl.ds(pl.multiple_of((1 - parity) * HALF + parts.low(group), 16), parts.sizes[group])
        return remote(out.at[rows], arriving.at[parts.rows(group)], swap_sem.at[0, group], swap_sem.at[1, group], other)

    opened_halves = set()

    def opened(group, kind):
        reduce.near_total(group, kind, finish)
        opened_halves.add((group, kind))
        if (group, 1 - kind) in opened_halves:
            swap(group).start()

    parts.run(
        [
            reduce.far_relays,
            reduce.far_directs,
            reduce.far_relay,
            reduce.far_total,
            reduce.near_relay,
            opened,
        ],
        SECOND_ORDER,
    )
    for group in range(parts.count):
        reduce.close(group)
        swap(group).wait()


def reduce_scratch(count):
    bf16 = jnp.bfloat16
    dma = pltpu.SemaphoreType.DMA
    return [
        pltpu.VMEM((2, 2, 2, HALF, VECS), bf16),
        pltpu.VMEM((2, SIDE, HALF, VECS), bf16),
        pltpu.VMEM((2, 6, 2, HALF, VECS), bf16),
        pltpu.VMEM((2, 3, HALF, VECS), bf16),
        dma((count, 2, 6)),
        dma((count, 2, 6)),
        dma((count, 2, 6)),
        dma((count, 2, 6)),
    ]


HBM = pl.BlockSpec(memory_space=pltpu.HBM)
VMEM = pl.BlockSpec(memory_space=pltpu.VMEM)
SCALAR = pl.BlockSpec(memory_space=pltpu.SMEM)


def comm_call(kernel, name, collective_id, limit, in_specs, out_shape, scratch):
    return pl.pallas_call(
        kernel,
        out_shape=out_shape,
        in_specs=in_specs,
        out_specs=jax.tree.map(lambda _: VMEM, out_shape),
        scratch_shapes=scratch,
        compiler_params=pltpu.CompilerParams(
            collective_id=collective_id, has_side_effects=True, vmem_limit_bytes=limit * 1024 * 1024
        ),
        name=name,
    )


def panel_shape(row_count):
    return jax.ShapeDtypeStruct((row_count, ROWS, VECS), jnp.bfloat16)


def gather_scratch(count):
    dma = pltpu.SemaphoreType.DMA
    return [dma((count, 2, 7)), dma((count, 2, 7))]


def gathered(row_ids, col_ids, start, values, row_count):
    return comm_call(
        gather_kernel,
        "gather_rows",
        0,
        LIMITS[0],
        [HBM, HBM, HBM, HBM],
        (
            panel_shape(row_count),
            jax.ShapeDtypeStruct(values.shape, values.dtype),
            jax.ShapeDtypeStruct(row_ids.shape, jnp.int32),
        ),
        [pltpu.VMEM(row_ids.shape, jnp.int32)] * 2
        + [pltpu.SemaphoreType.DMA((4,))]
        + gather_scratch(len(GATHER_PARTS)),
    )(*[pltpu.with_memory_space_constraint(value, pltpu.HBM) for value in (row_ids, col_ids, start, values)])


def first_of(center, width, terms, start, row_count):
    count = len(FIRST_PARTS)
    return comm_call(
        first_kernel,
        "reduce_and_gather",
        1,
        LIMITS[1],
        [SCALAR, SCALAR, VMEM, VMEM],
        panel_shape(row_count),
        gather_scratch(count) + reduce_scratch(count),
    )(center, width, terms.reshape(SIDE, SIDE, ROWS, VECS), start)


def second_of(center, width, terms, start, panel):
    count = len(SECOND_PARTS)
    return comm_call(
        second_kernel,
        "reduce_and_swap",
        2,
        LIMITS[2],
        [SCALAR, SCALAR, VMEM, VMEM, VMEM],
        (
            jax.ShapeDtypeStruct((ROWS, VECS), jnp.bfloat16),
            jax.ShapeDtypeStruct((HALF, VECS), jnp.bfloat16),
        ),
        [pltpu.SemaphoreType.DMA((2, count))] + reduce_scratch(count),
    )(center, width, terms.reshape(SIDE, SIDE, ROWS, VECS), start, panel)


LIMITS = (4, 22, 22)


def on_device(block_values, block_rows, block_cols, start_vectors, center, half_width, row_counts):
    values = block_values.reshape(-1, ORB, ORB)
    row_ids = block_rows.reshape(1, -1)
    col_ids = block_cols.reshape(1, -1)
    col_count = lax.axis_size("col")
    row_count = lax.axis_size("row")
    out_blocks = col_count * BD

    panel, values, codes = gathered(row_ids, col_ids, start_vectors, values, row_count)
    terms = cell_terms(codes, values, panel, out_blocks)
    panel = first_of(center, half_width, terms, start_vectors, row_count)
    terms = cell_terms(codes, values, panel, out_blocks)
    second, arriving = second_of(center, half_width, terms, start_vectors, panel)

    return placed_rows(row_counts, second, arriving)


UNIT = ORB // 2


def placing_kernel(counts_ref, second, arriving, out):
    device = lax.axis_index("row") * lax.axis_size("col") + lax.axis_index("col")
    parity = device % 2
    even_count = counts_ref[device - parity]
    live = 2 * counts_ref[device]
    first = parity * (2 * even_count - BD)

    @pl.loop(0, out.shape[0] // UNIT)
    def _(unit):
        at = first + unit
        here = pl.ds(pl.multiple_of(unit * UNIT, UNIT), UNIT)
        own_at = at - parity * BD
        other_at = at - (1 - parity) * 2 * BD
        is_own = jnp.logical_and(own_at >= 0, own_at < 2 * BD)
        is_live = unit < live

        @pl.when(jnp.logical_and(is_live, is_own))
        def _():
            out[here] = second[pl.ds(pl.multiple_of(own_at * UNIT, UNIT), UNIT)]

        @pl.when(jnp.logical_and(is_live, jnp.logical_not(is_own)))
        def _():
            out[here] = arriving[pl.ds(pl.multiple_of(other_at * UNIT, UNIT), UNIT)]

        @pl.when(jnp.logical_not(is_live))
        def _():
            out[here] = jnp.zeros((UNIT, VECS), jnp.bfloat16)


def placed_rows(row_counts, second, arriving):
    return pl.pallas_call(
        placing_kernel,
        out_shape=jax.ShapeDtypeStruct(((BD + MOVE) * ORB, VECS), jnp.bfloat16),
        in_specs=[SCALAR, VMEM, VMEM],
        out_specs=VMEM,
        compiler_params=pltpu.CompilerParams(vmem_limit_bytes=10 * 1024 * 1024),
        name="place_rows",
    )(row_counts, second, arriving)


def solution(mesh):
    placed = (
        P("row", "col", None, None, None),
        P("row", "col", None),
        P("row", "col", None),
        P(("row", "col"), None),
        P(),
        P(),
        P(),
    )
    return jax.shard_map(
        on_device, mesh=mesh, in_specs=placed, out_specs=P(("row", "col"), None), check_vma=False
    )
```

```python
import functools

import jax
import jax.numpy as jnp
from jax import lax
from jax.experimental import pallas as pl
from jax.experimental.pallas import tpu as pltpu
from jax.sharding import PartitionSpec as P

ORB = 128
VECS = 256
BD = 13
MOVE = 6
GROUP = 128


def product_kernel(codes_ref, values_ref, panel_ref, out_ref):
    @pl.loop(0, out_ref.shape[0] // 8)
    def _(i):
        out_ref[pl.ds(8 * i, 8)] = jnp.zeros((8, ORB, VECS), jnp.bfloat16)

    def group(step, carry):
        before, total = carry
        for e in range(GROUP):
            code = codes_ref[0, step * GROUP + e]
            row, col, entry = code >> 15, (code >> 8) & 127, code & 255
            product = jnp.dot(values_ref[entry], panel_ref[col], preferred_element_type=jnp.float32)
            total = jnp.where(row == before, total, 0.0) + product
            out_ref[row] = total.astype(jnp.bfloat16)
            before = row
        return before, total

    lax.fori_loop(
        0, values_ref.shape[0] // GROUP, group, (jnp.int32(-1), jnp.zeros((ORB, VECS), jnp.float32))
    )


def cell_terms(codes, values, panel_rows, out_blocks):
    panel = panel_rows.reshape(-1, ORB, VECS)
    vmem = pl.BlockSpec(memory_space=pltpu.VMEM)
    return pl.pallas_call(
        product_kernel,
        out_shape=jax.ShapeDtypeStruct((out_blocks, ORB, VECS), jnp.bfloat16),
        in_specs=[pl.BlockSpec(memory_space=pltpu.SMEM), vmem, vmem],
        out_specs=vmem,
        compiler_params=pltpu.CompilerParams(vmem_limit_bytes=PRODUCT_LIMIT * 1024 * 1024),
        name="block_products",
    )(codes, values, panel)


PRODUCT_LIMIT = 10
MESH = pl.DeviceIdType.MESH
SIDE = 4
HALF = BD * ORB // 2
ROWS = BD * ORB
GATHER_PARTS = (832,)
FIRST_PARTS = (256, 256, 192, 128)
SECOND_PARTS = (448, 384)
RELAY_A, RELAY_B, DIRECT_A, DIRECT_B, SUM_A, SUM_B = range(6)
FIRST_ORDER = (
    0, 1, 32, 33, 2, 3, 64, 65, 34, 35, 66, 67, 96, 97, 4, 5, 98, 128, 129, 99,
    36, 37, 68, 69, 161, 193, 130, 131, 160, 192, 225, 6, 7, 224, 38, 39, 257, 100, 256, 101,
    162, 194, 163, 195, 70, 71, 226, 133, 132, 227, 102, 103, 258, 164, 196, 259, 165, 197, 134, 135,
    166, 198, 228, 167, 199, 229, 230, 260, 231, 261, 262, 263,
)
SECOND_ORDER = (
    0, 1, 32, 33, 2, 3, 64, 65, 34, 35, 66, 67, 96, 97, 98, 99, 128, 129, 130, 131,
    160, 161, 162, 163,
)
STRIPE = 32


def shifted(position, by):
    return (position + by + SIDE) % SIDE


class Place:
    def __init__(self):
        self.row = lax.axis_index("row")
        self.col = lax.axis_index("col")
        self.z, self.core = self.row // 2, self.row % 2
        self.x, self.y = self.col // SIDE, self.col % SIDE

    def along(self, axis, by):
        if axis == 0:
            return (self.row, shifted(self.x, by) * SIDE + self.y)
        if axis == 1:
            return (self.row, self.x * SIDE + shifted(self.y, by))
        return (self.slot(by), self.col)

    def slot(self, by):
        return shifted(self.z, by) * 2 + self.core

    def partner(self):
        return (self.z * 2 + 1 - self.core, self.col)

    def greet(self, targets):
        barrier = pltpu.get_barrier_semaphore()
        for target in targets:
            pl.semaphore_signal(barrier, inc=1, device_id=target, device_id_type=MESH)
        pl.semaphore_wait(barrier, len(targets))


def remote(src, dst, send_sem, recv_sem, target):
    return pltpu.make_async_remote_copy(
        src_ref=src, dst_ref=dst, send_sem=send_sem, recv_sem=recv_sem, device_id=target, device_id_type=MESH
    )


class Parts:
    def __init__(self, sizes):
        self.sizes = sizes
        self.count = len(sizes)

    def low(self, group):
        return sum(self.sizes[:group])

    def near(self, group, half):
        size = self.sizes[group]
        first = size // 32 * 16 + size % 32
        return (self.low(group), first) if half == 0 else (self.low(group) + first, size - first)

    def rows(self, group):
        return pl.ds(self.low(group), self.sizes[group])

    def own(self, group, kind):
        return pl.ds(kind * HALF + self.low(group), self.sizes[group])

    def run(self, stages, order):
        for code in order:
            stages[code // 32](code % 32 // 2, code % 2)


def stripes(low, rows, body):
    @pl.loop(0, rows // STRIPE)
    def _(i):
        body(pl.multiple_of(low + i * STRIPE, STRIPE))


def wide(value):
    return value.astype(jnp.float32)


class Gather:
    def __init__(self, place, parts, panel, send_sem, recv_sem, own=None):
        self.place, self.parts, self.panel, self.own = place, parts, panel, own
        self.send_sem, self.recv_sem = send_sem, recv_sem

    def copy(self, group, kind, index):
        place = self.place
        rows = self.parts.own(group, kind)
        plus, minus, partner = place.along(2, 1), place.along(2, -1), place.partner()
        mine, below, above, far = place.slot(0), place.slot(-1), place.slot(1), place.slot(2)
        slot, target = [
            (mine, plus),
            (mine, minus),
            (mine, partner),
            (below, plus) if kind == 0 else (above, minus),
            (below, partner),
            (above, partner),
            (far, partner),
        ][index]
        block = self.panel.at[slot, rows]
        sems = (group, kind, index)
        source = self.own.at[rows] if self.own is not None and index < 3 else block
        return remote(source, block, self.send_sem.at[sems], self.recv_sem.at[sems], target)

    def neighbours(self):
        return [self.place.along(2, 1), self.place.along(2, -1), self.place.partner()]

    def first(self, group, kind):
        for index in range(3):
            self.copy(group, kind, index).start()

    def second(self, group, kind):
        self.copy(group, kind, kind).wait_recv()
        self.copy(group, kind, 3).start()
        self.copy(group, kind, 4 + kind).start()
        self.copy(group, kind, 1 - kind).wait_recv()
        self.copy(group, kind, 5 - kind).start()

    def third(self, group, kind):
        self.copy(group, kind, 3).wait_recv()
        self.copy(group, kind, 6).start()

    def close(self, group):
        for kind in range(2):
            for index in (2, 4, 5, 6):
                self.copy(group, kind, index).wait_recv()
            for index in range(7):
                self.copy(group, kind, index).wait_send()


def sorted_codes(rows_ref, cols_ref):
    count = rows_ref.shape[1]
    entry = lax.broadcasted_iota(jnp.int32, (1, count), 1)
    codes = wide((rows_ref[...] * 128 + cols_ref[...]) * 256 + entry)
    across = jnp.broadcast_to(codes, (count, count))
    down = across.T
    rank = jnp.sum(jnp.where(across < down, 1.0, 0.0), axis=1, keepdims=True)
    place = wide(lax.broadcasted_iota(jnp.int32, (count, count), 1))
    return jnp.sum(jnp.where(rank == place, down, 0.0), axis=0, keepdims=True).astype(jnp.int32)


def gather_kernel(rows_hbm, cols_hbm, start_hbm, values_hbm, panel, values, codes, rows_ref, cols_ref, load_sem, send_sem, recv_sem):
    place = Place()
    gather = Gather(place, Parts(GATHER_PARTS), panel, send_sem, recv_sem, start_hbm)
    load = pltpu.make_async_copy(start_hbm, panel.at[place.slot(0)], load_sem.at[0])
    values_load = pltpu.make_async_copy(values_hbm, values, load_sem.at[1])
    id_loads = [
        pltpu.make_async_copy(rows_hbm, rows_ref, load_sem.at[2]),
        pltpu.make_async_copy(cols_hbm, cols_ref, load_sem.at[3]),
    ]
    for id_load in id_loads:
        id_load.start()
    place.greet(gather.neighbours())
    for group in range(gather.parts.count):
        for kind in range(2):
            gather.first(group, kind)
    load.start()
    values_load.start()
    for id_load in id_loads:
        id_load.wait()
    codes[...] = sorted_codes(rows_ref, cols_ref)
    for group in range(gather.parts.count + 1):
        for kind in range(2):
            if group < gather.parts.count:
                gather.second(group, kind)
            if group > 0:
                gather.third(group - 1, kind)
    for group in range(gather.parts.count):
        gather.close(group)
    load.wait()
    values_load.wait()


class Reduce:
    def __init__(self, place, parts, terms, sums, result, far_slots, near_slots, far_send, far_recv, near_send, near_recv):
        self.place, self.parts, self.terms = place, parts, terms
        self.sums, self.result, self.far_slots, self.near_slots = sums, result, far_slots, near_slots
        self.far_sems, self.near_sems = (far_send, far_recv), (near_send, near_recv)

    def position(self, axis):
        return self.place.x if axis == 0 else self.place.y

    def piece(self, kind, target, half, rows):
        span = pl.ds(2 * half, 2)
        return (target, span, rows) if kind == 0 else (span, target, rows)

    def far(self, group, kind, index):
        p = self.position(kind)
        rows, own = self.parts.rows(group), self.parts.own(group, kind)
        by = -1 if index in (RELAY_A, DIRECT_B, SUM_A) else 1
        if index in (RELAY_A, RELAY_B):
            source = self.terms.at[self.piece(kind, shifted(p, 2), index - RELAY_A, own)]
        elif index == DIRECT_A:
            source = self.terms.at[self.piece(kind, shifted(p, 1), 0, own)]
        elif index == DIRECT_B:
            source = self.terms.at[self.piece(kind, shifted(p, -1), 1, own)]
        else:
            source = self.sums.at[index - SUM_A, kind, :, rows]
        sems = (group, kind, index)
        return remote(
            source,
            self.far_slots.at[kind, index, :, rows],
            self.far_sems[0].at[sems],
            self.far_sems[1].at[sems],
            self.place.along(kind, by),
        )

    def near_copy(self, group, kind, index):
        axis = 1 - kind
        p = self.position(axis)
        half, by, to = {
            RELAY_A: (0, -1, 2),
            RELAY_B: (1, 1, 2),
            DIRECT_B: (1, -1, -1),
            DIRECT_A: (0, 1, 1),
            SUM_A: (0, -1, -1),
            SUM_B: (1, 1, 1),
        }[index]
        rows = pl.ds(*self.parts.near(group, half))
        sems = (group, kind, index)
        return remote(
            self.result.at[kind, shifted(p, to), rows],
            self.near_slots.at[kind, index // 2, rows],
            self.near_sems[0].at[sems],
            self.near_sems[1].at[sems],
            self.place.along(axis, by),
        )

    def neighbours(self):
        return [self.place.along(axis, by) for axis in (0, 1) for by in (1, -1)]

    def far_relays(self, group, kind):
        self.far(group, kind, RELAY_A).start()
        self.far(group, kind, RELAY_B).start()

    def far_directs(self, group, kind):
        self.far(group, kind, DIRECT_A).start()
        self.far(group, kind, DIRECT_B).start()

    def far_relay(self, group, kind):
        p = self.position(kind)
        for side, (arrived, leaving, to) in enumerate(((RELAY_A, SUM_A, -1), (RELAY_B, SUM_B, 1))):
            self.far(group, kind, arrived).wait_recv()
            target = shifted(p, to)

            def body(at, side=side, arrived=arrived, target=target):
                rows = pl.ds(at, STRIPE)
                own = pl.ds(kind * HALF + at, STRIPE)
                self.sums[side, kind, :, rows] = (
                    self.terms[self.piece(kind, target, side, own)] + self.far_slots[kind, arrived, :, rows]
                )

            stripes(self.parts.low(group), self.parts.sizes[group], body)
            self.far(group, kind, leaving).start()

    def far_total(self, group, kind):
        p = self.position(kind)
        for index in (DIRECT_A, DIRECT_B, SUM_A, SUM_B):
            self.far(group, kind, index).wait_recv()

        def body(at):
            rows = pl.ds(at, STRIPE)
            own = pl.ds(kind * HALF + at, STRIPE)
            for half, (one, two) in enumerate(((DIRECT_A, SUM_A), (DIRECT_B, SUM_B))):
                value = (
                    wide(self.terms[self.piece(kind, p, half, own)])
                    + wide(self.far_slots[kind, one, :, rows])
                    + wide(self.far_slots[kind, two, :, rows])
                )
                self.result[kind, pl.ds(2 * half, 2), rows] = value.astype(jnp.bfloat16)

        stripes(self.parts.low(group), self.parts.sizes[group], body)
        for index in (RELAY_A, RELAY_B, DIRECT_A, DIRECT_B):
            self.near_copy(group, kind, index).start()

    def near_relay(self, group, kind):
        p = self.position(1 - kind)
        for half, (arrived, leaving, to) in enumerate(((RELAY_A, SUM_A, -1), (RELAY_B, SUM_B, 1))):
            self.near_copy(group, kind, arrived).wait_recv()
            target = shifted(p, to)

            def body(at, target=target):
                rows = pl.ds(at, STRIPE)
                self.result[kind, target, rows] += self.near_slots[kind, 0, rows]

            stripes(*self.parts.near(group, half), body)
            self.near_copy(group, kind, leaving).start()

    def near_total(self, group, kind, finish):
        p = self.position(1 - kind)
        for half, (one, two) in enumerate(((DIRECT_A, SUM_A), (DIRECT_B, SUM_B))):
            self.near_copy(group, kind, one).wait_recv()
            self.near_copy(group, kind, two).wait_recv()

            def body(at):
                rows = pl.ds(at, STRIPE)
                value = (
                    wide(self.result[kind, p, rows])
                    + wide(self.near_slots[kind, 1, rows])
                    + wide(self.near_slots[kind, 2, rows])
                )
                finish(pl.ds(kind * HALF + at, STRIPE), value)

            stripes(*self.parts.near(group, half), body)

    def close(self, group):
        for kind in range(2):
            for index in range(6):
                self.far(group, kind, index).wait_send()
                self.near_copy(group, kind, index).wait_send()


def first_kernel(center, width, terms, source, panel, gather_send, gather_recv, *scratch):
    place = Place()
    parts = Parts(FIRST_PARTS)
    gather = Gather(place, parts, panel, gather_send, gather_recv)
    reduce = Reduce(place, parts, terms, *scratch)
    place.greet(reduce.neighbours() + gather.neighbours())
    mine = place.slot(0)

    def finish(rows, image):
        value = (image - center[0] * wide(source[rows])) / width[0]
        panel[mine, rows] = value.astype(jnp.bfloat16)

    def opened(group, kind):
        reduce.near_total(group, kind, finish)

    parts.run(
        [
            reduce.far_relays,
            reduce.far_directs,
            reduce.far_relay,
            reduce.far_total,
            reduce.near_relay,
            opened,
            gather.first,
            gather.second,
            gather.third,
        ],
        FIRST_ORDER,
    )
    for group in range(parts.count):
        reduce.close(group)
        gather.close(group)


def second_kernel(center, width, terms, source, panel, out, arriving, swap_sem, *scratch):
    place = Place()
    parts = Parts(SECOND_PARTS)
    reduce = Reduce(place, parts, terms, *scratch)
    place.greet(reduce.neighbours())
    parity = place.y % 2
    other = (place.row, place.x * SIDE + place.y + 1 - 2 * parity)
    mine = place.slot(0)

    def finish(rows, image):
        value = 2.0 * (image - center[0] * wide(panel[mine, rows])) / width[0] - wide(source[rows])
        out[rows] = value.astype(jnp.bfloat16)

    def swap(group):
        rows = pl.ds(pl.multiple_of((1 - parity) * HALF + parts.low(group), 16), parts.sizes[group])
        return remote(out.at[rows], arriving.at[parts.rows(group)], swap_sem.at[0, group], swap_sem.at[1, group], other)

    opened_halves = set()

    def opened(group, kind):
        reduce.near_total(group, kind, finish)
        opened_halves.add((group, kind))
        if (group, 1 - kind) in opened_halves:
            swap(group).start()

    parts.run(
        [
            reduce.far_relays,
            reduce.far_directs,
            reduce.far_relay,
            reduce.far_total,
            reduce.near_relay,
            opened,
        ],
        SECOND_ORDER,
    )
    for group in range(parts.count):
        reduce.close(group)
        swap(group).wait()


def reduce_scratch(count):
    bf16 = jnp.bfloat16
    dma = pltpu.SemaphoreType.DMA
    return [
        pltpu.VMEM((2, 2, 2, HALF, VECS), bf16),
        pltpu.VMEM((2, SIDE, HALF, VECS), bf16),
        pltpu.VMEM((2, 6, 2, HALF, VECS), bf16),
        pltpu.VMEM((2, 3, HALF, VECS), bf16),
        dma((count, 2, 6)),
        dma((count, 2, 6)),
        dma((count, 2, 6)),
        dma((count, 2, 6)),
    ]


HBM = pl.BlockSpec(memory_space=pltpu.HBM)
VMEM = pl.BlockSpec(memory_space=pltpu.VMEM)
SCALAR = pl.BlockSpec(memory_space=pltpu.SMEM)


def comm_call(kernel, name, collective_id, limit, in_specs, out_shape, scratch):
    return pl.pallas_call(
        kernel,
        out_shape=out_shape,
        in_specs=in_specs,
        out_specs=jax.tree.map(lambda _: VMEM, out_shape),
        scratch_shapes=scratch,
        compiler_params=pltpu.CompilerParams(
            collective_id=collective_id, has_side_effects=True, vmem_limit_bytes=limit * 1024 * 1024
        ),
        name=name,
    )


def panel_shape(row_count):
    return jax.ShapeDtypeStruct((row_count, ROWS, VECS), jnp.bfloat16)


def gather_scratch(count):
    dma = pltpu.SemaphoreType.DMA
    return [dma((count, 2, 7)), dma((count, 2, 7))]


def gathered(row_ids, col_ids, start, values, row_count):
    return comm_call(
        gather_kernel,
        "gather_rows",
        0,
        LIMITS[0],
        [HBM, HBM, HBM, HBM],
        (
            panel_shape(row_count),
            jax.ShapeDtypeStruct(values.shape, values.dtype),
            jax.ShapeDtypeStruct(row_ids.shape, jnp.int32),
        ),
        [pltpu.VMEM(row_ids.shape, jnp.int32)] * 2
        + [pltpu.SemaphoreType.DMA((4,))]
        + gather_scratch(len(GATHER_PARTS)),
    )(*[pltpu.with_memory_space_constraint(value, pltpu.HBM) for value in (row_ids, col_ids, start, values)])


def first_of(center, width, terms, start, row_count):
    count = len(FIRST_PARTS)
    return comm_call(
        first_kernel,
        "reduce_and_gather",
        1,
        LIMITS[1],
        [SCALAR, SCALAR, VMEM, VMEM],
        panel_shape(row_count),
        gather_scratch(count) + reduce_scratch(count),
    )(center, width, terms.reshape(SIDE, SIDE, ROWS, VECS), start)


def second_of(center, width, terms, start, panel):
    count = len(SECOND_PARTS)
    return comm_call(
        second_kernel,
        "reduce_and_swap",
        2,
        LIMITS[2],
        [SCALAR, SCALAR, VMEM, VMEM, VMEM],
        (
            jax.ShapeDtypeStruct((ROWS, VECS), jnp.bfloat16),
            jax.ShapeDtypeStruct((HALF, VECS), jnp.bfloat16),
        ),
        [pltpu.SemaphoreType.DMA((2, count))] + reduce_scratch(count),
    )(center, width, terms.reshape(SIDE, SIDE, ROWS, VECS), start, panel)


LIMITS = (4, 22, 22)


def on_device(block_values, block_rows, block_cols, start_vectors, center, half_width, row_counts):
    values = block_values.reshape(-1, ORB, ORB)
    row_ids = block_rows.reshape(1, -1)
    col_ids = block_cols.reshape(1, -1)
    col_count = lax.axis_size("col")
    row_count = lax.axis_size("row")
    out_blocks = col_count * BD

    panel, values, codes = gathered(row_ids, col_ids, start_vectors, values, row_count)
    terms = cell_terms(codes, values, panel, out_blocks)
    panel = first_of(center, half_width, terms, start_vectors, row_count)
    terms = cell_terms(codes, values, panel, out_blocks)
    second, arriving = second_of(center, half_width, terms, start_vectors, panel)

    return placed_rows(row_counts, second, arriving)


UNIT = ORB // 2


def placing_kernel(counts_ref, second, arriving, out):
    device = lax.axis_index("row") * lax.axis_size("col") + lax.axis_index("col")
    parity = device % 2
    even_count = counts_ref[device - parity]
    live = 2 * counts_ref[device]
    first = parity * (2 * even_count - BD)

    @pl.loop(0, out.shape[0] // UNIT)
    def _(unit):
        at = first + unit
        here = pl.ds(pl.multiple_of(unit * UNIT, UNIT), UNIT)
        own_at = at - parity * BD
        other_at = at - (1 - parity) * 2 * BD
        is_own = jnp.logical_and(own_at >= 0, own_at < 2 * BD)
        is_live = unit < live

        @pl.when(jnp.logical_and(is_live, is_own))
        def _():
            out[here] = second[pl.ds(pl.multiple_of(own_at * UNIT, UNIT), UNIT)]

        @pl.when(jnp.logical_and(is_live, jnp.logical_not(is_own)))
        def _():
            out[here] = arriving[pl.ds(pl.multiple_of(other_at * UNIT, UNIT), UNIT)]

        @pl.when(jnp.logical_not(is_live))
        def _():
            out[here] = jnp.zeros((UNIT, VECS), jnp.bfloat16)


def placed_rows(row_counts, second, arriving):
    return pl.pallas_call(
        placing_kernel,
        out_shape=jax.ShapeDtypeStruct(((BD + MOVE) * ORB, VECS), jnp.bfloat16),
        in_specs=[SCALAR, VMEM, VMEM],
        out_specs=VMEM,
        compiler_params=pltpu.CompilerParams(vmem_limit_bytes=10 * 1024 * 1024),
        name="place_rows",
    )(row_counts, second, arriving)


def solution(mesh):
    placed = (
        P("row", "col", None, None, None),
        P("row", "col", None),
        P("row", "col", None),
        P(("row", "col"), None),
        P(),
        P(),
        P(),
    )
    return jax.shard_map(
        on_device, mesh=mesh, in_specs=placed, out_specs=P(("row", "col"), None), check_vma=False
    )
```
